512 devices in a mesh: section: 8 (over z_hi, x), expert: 64 (over z_lo, y, core).
Axes of the slice: x: 4, y: 4, z: 16 (z_hi: 2, z_lo: 8; z = z_hi * 8 + z_lo), core: 2. Of those that a mesh axis runs over, the one named last changes fastest.
Arguments:
- inputs: bfloat16 [4, 2048, 1536], P(None, 'expert', 'section'), may hold values from -36 to 36
- cotangent: bfloat16 [4, 2048, 1536], P(None, 'expert', 'section'), may hold values from -1.25 to 1.25
- expert_out: bfloat16 [8, 4, 128, 64, 2, 1536], P('section', None, 'expert'), may hold values from -6 to 6
- route_ids: int32 [8, 4, 2048, 4], P('section', None, 'expert'), may hold values from 0 to 127, all different within a row; in each aligned block of 32 rows (0 to 31, 32 to 63, ..., all dimensions but the last counted through in order) at most 2 rows name the same one
- router_w: bfloat16 [8, 1536, 128], P('section'), may hold values from -0.15625 to 0.15625
- norm_gain: float32 [8, 1536], P('section'), may hold values from 0.1 to 1.9
- final_gain: float32 [1536], replicated, may hold values from 0.1 to 1.9
Outputs:
- router_grad: float32 [8, 1536, 128], P('section', 'expert')
- gain_grad: float32 [8, 1536], P('section', 'expert')
The draws below stay inside these ranges and needn't reach their ends.
Inputs may be any that keep to these rules, and one draw needn't show every extreme that they name: `route_ids`: no expert is named by more than 2 of the 32 tokens that one device of the expert axis holds, in one layer and microbatch; some expert reaches it.
All inputs are finite; a program needn't handle non-finite values.
Results may differ from the reference program's by a relative error of at most 0.012.
Values may be sent and summed in bfloat16 or wider, within the bound.
No kernel may reach another device: no remote copies, remote signals or barrier semaphores. Data moves between devices by JAX's collectives and lax.ppermute only.
A program may use at most 64 MiB of HBM per device.

```python
import math
import jax
import jax.numpy as jnp
import numpy as np
from jax import lax

D = 1536
TOPK = 4
TOKO = 32
MICRO = 4
EXPERTS = 128
CAP = 2
TOKENS = 2048
LAYERS = 8
N_EXPERT = 64


def draw_inputs(key, part):
    first_key, second_key, third_key = jax.random.split(key, 3)
    full_shape = (MICRO, TOKENS, D)
    base_draw = jnp.clip(jax.random.normal(first_key, full_shape, jnp.float32), -4.0, 4.0)
    row_scale = jnp.exp(jax.random.uniform(second_key, (MICRO, TOKENS, 1), jnp.float32, math.log(0.3), math.log(3.0)))
    columns = jnp.exp(jax.random.uniform(third_key, (1, 1, D), jnp.float32, math.log(0.3), math.log(3.0)))
    return (base_draw * row_scale * columns).astype(jnp.bfloat16)


def draw_cotangent(key, part):
    first_key, second_key = jax.random.split(key, 2)
    full_shape = (MICRO, TOKENS, D)
    owners = TOKENS // TOKO
    owner_pos = (jnp.arange(TOKENS) // TOKO).astype(jnp.float32) / max(owners - 1, 1)
    columns = jnp.exp(jax.random.uniform(second_key, (1, 1, D), jnp.float32, math.log(0.4), math.log(4.0)))
    base_draw = jnp.clip(jax.random.normal(first_key, full_shape, jnp.float32), -4.0, 4.0)
    rise_factor = jnp.exp(math.log(3.0) * owner_pos)
    return (0.02 * base_draw * rise_factor[None, :, None] * columns).astype(jnp.bfloat16)


def block_levels(rng, shape, cuts, smallest, largest):
    def one(axis_at, blocks):
        heights = jax.random.uniform(jax.random.fold_in(jax.random.fold_in(rng, 6), axis_at), (blocks,), jnp.float32, smallest / len(cuts), largest / len(cuts))
        return jnp.repeat(jnp.exp(heights), shape[axis_at] // blocks).reshape((-1,) + (1,) * (len(shape) - axis_at - 1))

    gain = one(*cuts[0])
    for cut in cuts[1:]:
        gain = gain * one(*cut)
    return gain


def shared_out(key, own, number, rows, amount, top, most, skew):
    sequence = jax.random.permutation(key, amount)
    crowded, usual = portions_of(amount, rows * top, most, skew, True), portions_of(amount, rows * top, most, skew, False)
    places = jnp.arange(amount)

    def named(tallies, rotation):
        used = int((tallies > 0).sum())
        fixed = max(1, used // 4)
        moved = fixed + (places - fixed + rotation * (used - fixed)) % max(1, amount - fixed)
        return jnp.zeros((amount,), jnp.int32).at[sequence[jnp.where(places < fixed, places, moved)]].set(jnp.asarray(tallies, jnp.int32))

    tallies = jnp.where(number % 4 == 0, named(crowded, number // 4), named(usual, number - number // 4 - 1))
    mixed = jax.random.permutation(jax.random.fold_in(own, 3), amount)
    giver, sink = mixed[0:amount // 2 * 2:2], mixed[1:amount // 2 * 2:2]
    room = jnp.minimum(tallies[giver] - 1, most - tallies[sink]) // 2
    room = jnp.where((giver == sequence[0]) | (sink == sequence[0]) | (tallies[sink] == 0), 0, jnp.maximum(room, 0))
    moved = jax.random.randint(jax.random.fold_in(own, 4), (amount // 2,), 0, 1 << 20) % (room + 1)
    tallies = tallies.at[giver].add(-moved).at[sink].add(moved)
    members = jnp.searchsorted(jnp.cumsum(tallies), jnp.arange(rows * top), side="right").astype(jnp.int32)
    grid = members.reshape(top, rows).T
    grid = grid[jax.random.permutation(jax.random.fold_in(own, 1), rows)]
    rotation = jax.random.randint(jax.random.fold_in(own, 2), (rows, 1), 0, top)
    return jnp.take_along_axis(grid, (jnp.arange(top)[None, :] + rotation) % top, axis=1)


def portions_of(amount, total, limit, lean, full):
    portions = [(1 << 20) // math.isqrt(standing ** lean) + 1 for standing in range(1, amount + 1)]
    largest = limit if full else min(limit, max(-(-total // amount), total * portions[0] // sum(portions)))
    least = 1 if total - largest >= amount - 1 else 0
    given, spare = [largest] + [least] * (amount - 1), total - largest - least * (amount - 1)
    while spare > 0:
        candidates = [i for i in range(1, amount) if given[i] < largest] or [i for i in range(1, amount) if given[i] < limit]
        pool, left = sum([portions[i] for i in candidates]), spare
        for i in candidates:
            extra = min(limit - given[i], max(1, left * portions[i] // pool), spare)
            given[i] = given[i] + extra
            spare = spare - extra
    return np.array(given)


def centred(key, extent, spread, bound, cuts=(), kind=jnp.bfloat16):
    factor_of = block_levels(key, extent, cuts, -0.22, 0.18) if cuts else 1.0
    entries = jax.random.normal(key, extent, jnp.float32) * spread * factor_of
    return jnp.minimum(jnp.maximum(entries, -bound), bound).astype(kind)


def setup_inputs(seed: int = 0) -> dict:
    arg_keys = jax.random.split(jax.random.key(seed), 8)
    inputs = draw_inputs(jax.random.fold_in(arg_keys[7], 71), 0)
    cotangent = draw_cotangent(jax.random.fold_in(arg_keys[7], 71), 0)
    expert_out = centred(arg_keys[2], (LAYERS, MICRO, EXPERTS, N_EXPERT, CAP, D), 1.0, 6.0, ((0, 8), (2, 64)))
    route_ids_keys = jax.random.split(jax.random.fold_in(arg_keys[3], 1), LAYERS * MICRO * TOKENS // TOKO)
    route_ids_turns = jax.random.permutation(jax.random.fold_in(arg_keys[3], 3), LAYERS * MICRO * TOKENS // TOKO)
    route_ids = jax.vmap(lambda own, number: shared_out(jax.random.fold_in(arg_keys[3], 2), own, number, TOKO, EXPERTS, TOPK, CAP, 2))(route_ids_keys, route_ids_turns).reshape((LAYERS, MICRO, TOKENS, TOPK))
    router_w = centred(arg_keys[4], (LAYERS, D, EXPERTS), D ** -0.5, 0.15625, ((0, 8),))
    norm_gain = jnp.clip(1.0 + 0.18 * jax.random.normal(arg_keys[5], (LAYERS, D), jnp.float32), 0.1, 1.9)
    final_gain = jnp.clip(1.0 + 0.18 * jax.random.normal(arg_keys[6], (D,), jnp.float32), 0.1, 1.9)
    return dict(inputs=inputs, cotangent=cotangent, expert_out=expert_out, route_ids=route_ids, router_w=router_w, norm_gain=norm_gain, final_gain=final_gain)


EPSILON = 1e-05

def rms_scale(values):
    return lax.rsqrt(lax.optimization_barrier(jnp.mean(values * values, axis=-1, keepdims=True)) + EPSILON)

def slot_numbers(route_layer):
    owners = TOKENS // TOKO
    pair_count = TOKO * TOPK
    blocks = route_layer.reshape(MICRO, owners, pair_count)
    matches = blocks[:, :, :, None] == blocks[:, :, None, :]
    earlier = lax.broadcasted_iota(jnp.int32, (pair_count, pair_count), 1) < lax.broadcasted_iota(jnp.int32, (pair_count, pair_count), 0)
    slot_index = lax.optimization_barrier(jnp.sum(jnp.where(matches & earlier, 1, 0), axis=-1)).astype(jnp.int32)
    return slot_index.reshape(MICRO, TOKENS, TOPK)

def picked_rows(expert_layer, route_layer):
    owners = TOKENS // TOKO
    slot_index = slot_numbers(route_layer)
    owner_of = (jnp.arange(TOKENS, dtype=jnp.int32) // TOKO)[None, :, None]
    row_index = ((route_layer * owners + owner_of) * CAP + slot_index).astype(jnp.int32).reshape(MICRO, TOKENS * TOPK)
    row_table = expert_layer.reshape(MICRO, EXPERTS * owners * CAP, D)
    gathered = jax.vmap(lambda block_table, block_rows: jnp.take(block_table, block_rows, axis=0))(row_table, row_index)
    return gathered.reshape(MICRO, TOKENS, TOPK, D)

def route_weights(normed, router_layer, route_layer):
    logits = jnp.dot(normed.reshape(MICRO * TOKENS, D), router_layer, preferred_element_type=jnp.float32)
    logits = logits.reshape(MICRO, TOKENS, EXPERTS)
    chosen = jnp.take_along_axis(logits, route_layer, axis=-1)
    raised = jnp.exp(chosen)
    return raised / lax.optimization_barrier(jnp.sum(raised, axis=-1, keepdims=True))

def forward_layer(state_rows, expert_layer, route_layer, router_layer, gain_layer):
    state_float = state_rows.astype(jnp.float32)
    rscale = rms_scale(state_float)
    normed = (state_float * rscale * gain_layer).astype(jnp.bfloat16)
    weights = route_weights(normed, router_layer, route_layer)
    picked = picked_rows(expert_layer, route_layer).astype(jnp.float32)
    mixture = lax.optimization_barrier(jnp.sum(weights[:, :, :, None] * picked, axis=2))
    return (state_float + mixture).astype(jnp.bfloat16)

def backward_layer(back_rows, state_rows, expert_layer, route_layer, router_layer, gain_layer):
    state_float = state_rows.astype(jnp.float32)
    rscale = rms_scale(state_float)
    normal_part = state_float * rscale
    normed = (normal_part * gain_layer).astype(jnp.bfloat16)
    weights = route_weights(normed, router_layer, route_layer)
    picked = picked_rows(expert_layer, route_layer).astype(jnp.float32)
    back_float = back_rows.astype(jnp.float32)
    dweights = lax.optimization_barrier(jnp.sum(back_float[:, :, None, :] * picked, axis=-1))
    dselect = weights * (dweights - lax.optimization_barrier(jnp.sum(weights * dweights, axis=-1, keepdims=True)))
    onehot = (route_layer[:, :, :, None] == jnp.arange(EXPERTS, dtype=jnp.int32)).astype(jnp.float32)
    dlogits = lax.optimization_barrier(jnp.sum(dselect[:, :, :, None] * onehot, axis=2)).astype(jnp.bfloat16)
    flat_normed = normed.reshape(MICRO * TOKENS, D)
    flat_dlogits = dlogits.reshape(MICRO * TOKENS, EXPERTS)
    router_term = jnp.dot(flat_normed.T, flat_dlogits, preferred_element_type=jnp.float32)
    dnormed = jnp.dot(flat_dlogits, router_layer.T, preferred_element_type=jnp.float32).reshape(MICRO, TOKENS, D)
    gain_term = lax.optimization_barrier(jnp.sum(dnormed * normal_part, axis=(0, 1)))
    varied = dnormed * gain_layer
    new_back = back_float + rscale * (varied - normal_part * lax.optimization_barrier(jnp.mean(varied * normal_part, axis=-1, keepdims=True)))
    return (new_back.astype(jnp.bfloat16), router_term, gain_term)

def reference(inputs, cotangent, expert_out, route_ids, router_w, norm_gain, final_gain):
    states = [inputs]
    for layer_num in range(LAYERS):
        states.append(forward_layer(states[-1], expert_out[layer_num], route_ids[layer_num], router_w[layer_num], norm_gain[layer_num]))
    last_float = states[-1].astype(jnp.float32)
    rscale = rms_scale(last_float)
    normal_part = last_float * rscale
    varied = cotangent.astype(jnp.float32) * final_gain
    back_rows = (rscale * (varied - normal_part * lax.optimization_barrier(jnp.mean(varied * normal_part, axis=-1, keepdims=True)))).astype(jnp.bfloat16)
    router_list = []
    gain_list = []
    for layer_num in reversed(range(LAYERS)):
        back_rows, router_term, gain_term = backward_layer(back_rows, states[layer_num], expert_out[layer_num], route_ids[layer_num], router_w[layer_num], norm_gain[layer_num])
        router_list.insert(0, router_term)
        gain_list.insert(0, gain_term)
    return (jnp.stack(router_list), jnp.stack(gain_list))
```

```python
import functools

import jax
import jax.numpy as jnp
from jax import lax
from jax.experimental import pallas as pl
from jax.experimental.pallas import tpu as pltpu
from jax.sharding import Mesh, PartitionSpec as P

EPSILON = 1e-05
HALVES = 2
F32 = jnp.float32
BF16 = jnp.bfloat16


def onehots(routes_ref, layer, choices, experts):
    lanes = lax.broadcasted_iota(jnp.int32, (routes_ref.shape[1], experts), 1)
    rows = routes_ref[layer]
    return [rows[:, k : k + 1] == lanes for k in range(choices)]


def forward_layer(layer, state, refs, normed_ref, weights_ref, rscale_ref):
    picks_ref, routes_ref, w_ref, gain_ref = refs
    half = state[0].shape[1]
    experts = w_ref.shape[2]
    choices = routes_ref.shape[2]
    floats = [part.astype(F32) for part in state]
    total = sum(jnp.sum(part * part, axis=-1, keepdims=True) for part in floats)
    rscale = lax.rsqrt(total / (HALVES * half) + EPSILON)
    logits = jnp.zeros((state[0].shape[0], experts), F32)
    for h in range(HALVES):
        normed = (floats[h] * rscale * gain_ref[layer, h : h + 1, :]).astype(BF16)
        normed_ref[layer, h] = normed
        logits += jnp.dot(normed, w_ref[layer, h * half : (h + 1) * half, :], preferred_element_type=F32)
    hots = onehots(routes_ref, layer, choices, experts)
    raised = [jnp.exp(jnp.sum(jnp.where(hot, logits, 0.0), axis=-1, keepdims=True)) for hot in hots]
    bottom = sum(raised)
    weights = [value / bottom for value in raised]
    for k in range(choices):
        weights_ref[layer, k] = jnp.broadcast_to(weights[k], weights_ref.shape[2:])
    rscale_ref[layer] = jnp.broadcast_to(rscale, rscale_ref.shape[1:])
    fresh = []
    for h in range(HALVES):
        mixture = sum(weights[k] * picks_ref[layer, h, k].astype(F32) for k in range(choices))
        fresh.append((floats[h] + mixture).astype(BF16))
    return fresh


def backward_layer(layer, back, state, refs, weights_ref, rscale_ref, dlogits_ref):
    picks_ref, routes_ref, w_ref, gain_ref = refs
    half = state[0].shape[1]
    experts = w_ref.shape[2]
    choices = routes_ref.shape[2]
    back_float = [part.astype(F32) for part in back]
    weights = [weights_ref[layer, k][:, 0:1] for k in range(choices)]
    rscale = rscale_ref[layer][:, 0:1]
    dweights = [
        sum(
            jnp.sum(back_float[h] * picks_ref[layer, h, k].astype(F32), axis=-1, keepdims=True)
            for h in range(HALVES)
        )
        for k in range(choices)
    ]
    average = sum(w * d for w, d in zip(weights, dweights))
    dlogits = jnp.zeros((back[0].shape[0], experts), F32)
    for k, hot in enumerate(onehots(routes_ref, layer, choices, experts)):
        dlogits += jnp.where(hot, weights[k] * (dweights[k] - average), 0.0)
    dlogits = dlogits.astype(BF16)
    dlogits_ref[layer] = dlogits
    varied, normal = [], []
    for h in range(HALVES):
        dnormed = lax.dot_general(
            dlogits,
            w_ref[layer, h * half : (h + 1) * half, :],
            (((1,), (1,)), ((), ())),
            preferred_element_type=F32,
        )
        varied.append(dnormed * gain_ref[layer, h : h + 1, :])
        normal.append(state[h].astype(F32) * rscale)
    mean = sum(jnp.sum(v * s, axis=-1, keepdims=True) for v, s in zip(varied, normal)) / (HALVES * half)
    return [(b + rscale * (v - s * mean)).astype(BF16) for b, v, s in zip(back_float, varied, normal)]


def first_kernel(
    zh_ref, table_ref, select_ref, routes_ref, w_ref, gain_ref, acts_ref,
    picks_ref, states_ref, normed_ref, weights_ref, rscale_ref, out_ref,
):
    layers = table_ref.shape[0]
    choices = routes_ref.shape[2]
    tokens = routes_ref.shape[1]
    for layer in range(layers):
        rows = jnp.dot(select_ref[layer], table_ref[layer], preferred_element_type=F32).astype(BF16)
        for h in range(HALVES):
            for k in range(choices):
                at = (h * choices + k) * tokens
                picks_ref[layer, h, k] = rows[at : at + tokens]

    @pl.when(zh_ref[0] == 0)
    def _():
        refs = (picks_ref, routes_ref, w_ref, gain_ref)
        state = [acts_ref[h] for h in range(HALVES)]
        for layer in range(layers):
            for h in range(HALVES):
                states_ref[layer, h] = state[h]
            state = forward_layer(layer, state, refs, normed_ref, weights_ref, rscale_ref)
        for h in range(HALVES):
            out_ref[h] = state[h]


def middle_kernel(
    zh_ref, arrived_ref, acts_ref, final_ref, picks_ref, routes_ref, w_ref, gain_ref, given_ref,
    normed_ref, dlogits_ref, out_ref, states_ref, weights_ref, rscale_ref,
):
    layers = picks_ref.shape[0]
    half = acts_ref.shape[2]

    @pl.when(zh_ref[0] == 0)
    def _():
        normed_ref[...] = given_ref[...]

    @pl.when(zh_ref[0] != 0)
    def _():
        refs = (picks_ref, routes_ref, w_ref, gain_ref)
        state = [arrived_ref[h] for h in range(HALVES)]
        for layer in range(layers):
            for h in range(HALVES):
                states_ref[layer, h] = state[h]
            state = forward_layer(layer, state, refs, normed_ref, weights_ref, rscale_ref)
        floats = [part.astype(F32) for part in state]
        total = sum(jnp.sum(part * part, axis=-1, keepdims=True) for part in floats)
        rscale = lax.rsqrt(total / (HALVES * half) + EPSILON)
        normal = [part * rscale for part in floats]
        varied = [acts_ref[h].astype(F32) * final_ref[h : h + 1, :] for h in range(HALVES)]
        mean = sum(jnp.sum(v * s, axis=-1, keepdims=True) for v, s in zip(varied, normal)) / (HALVES * half)
        back = [(rscale * (v - s * mean)).astype(BF16) for v, s in zip(varied, normal)]
        for layer in reversed(range(layers)):
            state = [states_ref[layer, h] for h in range(HALVES)]
            back = backward_layer(layer, back, state, refs, weights_ref, rscale_ref, dlogits_ref)
        for h in range(HALVES):
            out_ref[h] = back[h]


def last_kernel(
    zh_ref, arrived_ref, states_ref, weights_ref, rscale_ref, picks_ref, routes_ref, w_ref, gain_ref,
    given_ref, dlogits_ref,
):
    layers = picks_ref.shape[0]

    @pl.when(zh_ref[0] != 0)
    def _():
        dlogits_ref[...] = given_ref[...]

    @pl.when(zh_ref[0] == 0)
    def _():
        refs = (picks_ref, routes_ref, w_ref, gain_ref)
        back = [arrived_ref[h] for h in range(HALVES)]
        for layer in reversed(range(layers)):
            state = [states_ref[layer, h] for h in range(HALVES)]
            back = backward_layer(layer, back, state, refs, weights_ref, rscale_ref, dlogits_ref)


def grad_kernel(planes, normed_ref, dlogits_ref, out_ref):
    micros, _, tokens, half = normed_ref.shape
    experts = dlogits_ref.shape[2]
    groups, per_group = out_ref.shape[:2]
    piece = per_group // planes
    dlogits = dlogits_ref[...].reshape(micros * tokens, experts)
    for h in range(HALVES):
        rows = jnp.concatenate([normed_ref[m, h] for m in range(micros)], axis=0)
        term = lax.dot_general(rows, dlogits, (((0,), (0,)), ((), ())), preferred_element_type=F32)
        for at in range(0, half, piece):
            owner = (h * half + at) // piece
            plane, group = owner // groups, owner % groups
            out_ref[group, plane * piece : (plane + 1) * piece, :] = term[at : at + piece]


def call(kernel, outs, args, scratch=(), scalars=1):
    smem = [pl.BlockSpec(memory_space=pltpu.SMEM)] * scalars
    vmem = pl.BlockSpec(memory_space=pltpu.VMEM)
    return pl.pallas_call(
        kernel,
        out_shape=outs,
        in_specs=smem + [vmem] * (len(args) - scalars),
        out_specs=jax.tree.map(lambda _: vmem, outs),
        scratch_shapes=list(scratch),
    )(*args)


def slot_numbers(routes):
    flattened = routes.reshape(routes.shape[0], -1)
    pair_count = flattened.shape[1]
    matches = flattened[:, :, None] == flattened[:, None, :]
    earlier = lax.broadcasted_iota(jnp.int32, (pair_count, pair_count), 1) < lax.broadcasted_iota(
        jnp.int32, (pair_count, pair_count), 0
    )
    return jnp.sum(jnp.where(matches & earlier[None], 1, 0), axis=-1).astype(jnp.int32).reshape(routes.shape)


def thirds(values):
    high = values.astype(BF16)
    rest = values - high.astype(F32)
    middle = rest.astype(BF16)
    return jnp.stack([high, middle, (rest - middle.astype(F32)).astype(BF16)])


def per_device(expert_axes, plane_axis, flat_axes, inputs, cotangent, expert_out, route_ids, router_w, norm_gain, final_gain):
    zh = lax.axis_index("zh")
    micros, tokens, piece = inputs.shape
    layers = lax.axis_size("x")
    owners = lax.axis_size(expert_axes)
    local_experts, capacity, width = expert_out.shape[2], expert_out.shape[4], expert_out.shape[5]
    half = width // HALVES
    experts = router_w.shape[2]
    choices = route_ids.shape[3]
    zh_word = jnp.reshape(zh, (1,)).astype(jnp.int32)

    kept = jnp.where(zh == 0, inputs, cotangent)
    crossing = jnp.where(zh == 0, cotangent, inputs)
    crossed = lax.ppermute(crossing, "zh", [(0, 1), (1, 0)])

    rows = expert_out[0].reshape(micros, local_experts, owners, capacity, HALVES, half)
    rows = rows.transpose(0, 2, 1, 4, 3, 5).reshape(micros * owners, local_experts * HALVES * capacity, half)
    with jax.named_scope("rows_exchange"):
        table = lax.all_to_all(rows, ("x",) + expert_axes, split_axis=0, concat_axis=0, tiled=True)
    table = table.reshape(layers, experts * HALVES * capacity, half)

    lower = jnp.where(zh == 0, kept, crossed)
    upper = jnp.where(zh == 0, crossed, kept)
    acts_part = jnp.stack([lower, upper], axis=2).reshape(micros, tokens * HALVES * piece // 128, 128)
    act_rows = acts_part.shape[1]
    route_part = route_ids[0].astype(BF16).reshape(micros, tokens * choices // 128, 128)
    route_rows = route_part.shape[1]
    route_part = jnp.pad(route_part, ((0, 0), (0, 8 - route_rows), (0, 0)))
    gain_part = thirds(norm_gain[0]).reshape(3 * width // 128, 128)
    gain_rows = gain_part.shape[0]
    gain_part = jnp.pad(gain_part, ((0, -gain_rows % 8), (0, 0)))
    shared = jnp.concatenate([router_w[0], gain_part], axis=0)
    shared = jnp.broadcast_to(shared[None], (layers,) + shared.shape)
    with jax.named_scope("small_exchange"):
        packed = lax.all_to_all(
            jnp.concatenate([shared, acts_part, route_part], axis=1), "x", split_axis=0, concat_axis=0, tiled=True
        )
    w_all = packed[:, :width]
    gain_all = packed[:, width : width + gain_rows].reshape(layers, 3, width).astype(F32)
    gain_all = (gain_all[:, 0] + gain_all[:, 1] + gain_all[:, 2]).reshape(layers, HALVES, half)
    at = shared.shape[1]
    acts = packed[:, at : at + act_rows].reshape(layers, tokens, HALVES, piece)
    acts = acts.transpose(2, 1, 0, 3).reshape(HALVES, tokens, half)
    at += act_rows
    routes = packed[:, at : at + route_rows].reshape(layers, tokens, choices).astype(F32).astype(jnp.int32)

    target = routes * (HALVES * capacity) + slot_numbers(routes)
    target = target.transpose(0, 2, 1)[:, None] + (jnp.arange(HALVES) * capacity)[None, :, None, None]
    target = target.reshape(layers, HALVES * choices * tokens, 1)
    select = (target == jnp.arange(experts * HALVES * capacity)[None, None, :]).astype(BF16)

    shape = jax.ShapeDtypeStruct
    rows_shape = (HALVES, tokens, half)
    picks, states, normed, weights, rscale, sent = call(
        first_kernel,
        (
            shape((layers, HALVES, choices, tokens, half), BF16),
            shape((layers,) + rows_shape, BF16),
            shape((layers,) + rows_shape, BF16),
            shape((layers, choices, tokens, 128), F32),
            shape((layers, tokens, 128), F32),
            shape(rows_shape, BF16),
        ),
        (zh_word, table, select, routes, w_all, gain_all, acts),
    )
    arrived = lax.ppermute(sent, "zh", [(0, 1)])
    normed, dlogits, sent = call(
        middle_kernel,
        (
            shape((layers,) + rows_shape, BF16),
            shape((layers, tokens, experts), BF16),
            shape(rows_shape, BF16),
        ),
        (zh_word, arrived, acts, final_gain.reshape(HALVES, half), picks, routes, w_all, gain_all, normed),
        scratch=(
            pltpu.VMEM((layers,) + rows_shape, BF16),
            pltpu.VMEM((layers, choices, tokens, 128), F32),
            pltpu.VMEM((layers, tokens, 128), F32),
        ),
    )
    arrived = lax.ppermute(sent, "zh", [(1, 0)])
    with jax.named_scope("normed_exchange"):
        normed = lax.all_to_all(normed, "x", split_axis=0, concat_axis=0, tiled=True)
    dlogits = call(
        last_kernel,
        shape((layers, tokens, experts), BF16),
        (zh_word, arrived, states, weights, rscale, picks, routes, w_all, gain_all, dlogits),
    )
    dlogits = lax.all_to_all(dlogits, "x", split_axis=0, concat_axis=0, tiled=True)

    planes = lax.axis_size(plane_axis)
    groups = owners // planes
    term = call(
        functools.partial(grad_kernel, planes),
        shape((groups, width // groups, experts), F32),
        (normed, dlogits),
        scalars=0,
    )
    term = lax.all_to_all(term, flat_axes, split_axis=0, concat_axis=0, tiled=True)
    term = jnp.sum(term, axis=0).reshape(planes, width // owners, experts)
    term = lax.all_to_all(term, plane_axis, split_axis=0, concat_axis=0, tiled=True)
    router_part = jnp.sum(term, axis=0)
    at = lax.axis_index(expert_axes) * (width // owners)
    w_slab = lax.dynamic_slice_in_dim(router_w[0], at, width // owners, 0).astype(F32)
    gain_slab = lax.dynamic_slice_in_dim(norm_gain[0], at, width // owners, 0)
    gain_part = jnp.sum(w_slab * router_part, axis=-1) / gain_slab
    return (router_part[None], gain_part[None])


def solution(mesh):
    sections, owners = mesh.shape["section"], mesh.shape["expert"]
    planes = 8 if owners % 8 == 0 and owners > 8 else owners // 2
    groups = owners // planes
    wide = Mesh(mesh.devices.reshape(HALVES, sections // HALVES, planes, groups), ("zh", "x", "z", "yc"))
    section, expert = ("zh", "x"), ("z", "yc")
    placed = (
        P(None, expert, section),
        P(None, expert, section),
        P(section, None, expert, None, None, None),
        P(section, None, expert, None),
        P(section, None, None),
        P(section, None),
        P(),
    )
    return jax.shard_map(
        functools.partial(per_device, expert, "z", "yc"),
        mesh=wide,
        in_specs=placed,
        out_specs=(P(section, expert, None), P(section, expert)),
        check_vma=False,
    )
```

```python
import functools

import jax
import jax.numpy as jnp
from jax import lax
from jax.experimental import pallas as pl
from jax.experimental.pallas import tpu as pltpu
from jax.sharding import Mesh, PartitionSpec as P


EPSILON = 1e-05
HALVES = 2
F32 = jnp.float32
BF16 = jnp.bfloat16


def onehots(routes_ref, layer, choices, experts):
    lanes = lax.broadcasted_iota(jnp.int32, (routes_ref.shape[1], experts), 1)
    rows = routes_ref[layer]
    return [rows[:, k : k + 1] == lanes for k in range(choices)]


def forward_layer(layer, state, refs, normed_ref, weights_ref, rscale_ref):
    picks_ref, routes_ref, w_ref, gain_ref = refs
    half = state[0].shape[1]
    experts = w_ref.shape[2]
    choices = routes_ref.shape[2]
    floats = [part.astype(F32) for part in state]
    total = sum(jnp.sum(part * part, axis=-1, keepdims=True) for part in floats)
    rscale = lax.rsqrt(total / (HALVES * half) + EPSILON)
    logits = jnp.zeros((state[0].shape[0], experts), F32)
    for h in range(HALVES):
        normed = (floats[h] * rscale * gain_ref[layer, h : h + 1, :]).astype(BF16)
        normed_ref[layer, h] = normed
        logits += jnp.dot(normed, w_ref[layer, h * half : (h + 1) * half, :], preferred_element_type=F32)
    hots = onehots(routes_ref, layer, choices, experts)
    raised = [jnp.exp(jnp.sum(jnp.where(hot, logits, 0.0), axis=-1, keepdims=True)) for hot in hots]
    bottom = sum(raised)
    weights = [value / bottom for value in raised]
    for k in range(choices):
        weights_ref[layer, k] = jnp.broadcast_to(weights[k], weights_ref.shape[2:])
    rscale_ref[layer] = jnp.broadcast_to(rscale, rscale_ref.shape[1:])
    fresh = []
    for h in range(HALVES):
        mixture = sum(weights[k] * picks_ref[layer, h, k].astype(F32) for k in range(choices))
        fresh.append((floats[h] + mixture).astype(BF16))
    return fresh


def backward_layer(layer, back, state, refs, weights_ref, rscale_ref, dlogits_ref):
    picks_ref, routes_ref, w_ref, gain_ref = refs
    half = state[0].shape[1]
    experts = w_ref.shape[2]
    choices = routes_ref.shape[2]
    back_float = [part.astype(F32) for part in back]
    weights = [weights_ref[layer, k][:, 0:1] for k in range(choices)]
    rscale = rscale_ref[layer][:, 0:1]
    dweights = [
        sum(
            jnp.sum(back_float[h] * picks_ref[layer, h, k].astype(F32), axis=-1, keepdims=True)
            for h in range(HALVES)
        )
        for k in range(choices)
    ]
    average = sum(w * d for w, d in zip(weights, dweights))
    dlogits = jnp.zeros((back[0].shape[0], experts), F32)
    for k, hot in enumerate(onehots(routes_ref, layer, choices, experts)):
        dlogits += jnp.where(hot, weights[k] * (dweights[k] - average), 0.0)
    dlogits = dlogits.astype(BF16)
    dlogits_ref[layer] = dlogits
    varied, normal = [], []
    for h in range(HALVES):
        dnormed = lax.dot_general(
            dlogits,
            w_ref[layer, h * half : (h + 1) * half, :],
            (((1,), (1,)), ((), ())),
            preferred_element_type=F32,
        )
        varied.append(dnormed * gain_ref[layer, h : h + 1, :])
        normal.append(state[h].astype(F32) * rscale)
    mean = sum(jnp.sum(v * s, axis=-1, keepdims=True) for v, s in zip(varied, normal)) / (HALVES * half)
    return [(b + rscale * (v - s * mean)).astype(BF16) for b, v, s in zip(back_float, varied, normal)]


def first_kernel(
    zh_ref, table_ref, select_ref, routes_ref, w_ref, gain_ref, acts_ref,
    picks_ref, states_ref, normed_ref, weights_ref, rscale_ref, out_ref,
):
    layers = table_ref.shape[0]
    choices = routes_ref.shape[2]
    tokens = routes_ref.shape[1]
    for layer in range(layers):
        rows = jnp.dot(select_ref[layer], table_ref[layer], preferred_element_type=F32).astype(BF16)
        for h in range(HALVES):
            for k in range(choices):
                at = (h * choices + k) * tokens
                picks_ref[layer, h, k] = rows[at : at + tokens]

    @pl.when(zh_ref[0] == 0)
    def _():
        refs = (picks_ref, routes_ref, w_ref, gain_ref)
        state = [acts_ref[h] for h in range(HALVES)]
        for layer in range(layers):
            for h in range(HALVES):
                states_ref[layer, h] = state[h]
            state = forward_layer(layer, state, refs, normed_ref, weights_ref, rscale_ref)
        for h in range(HALVES):
            out_ref[h] = state[h]


def middle_kernel(
    zh_ref, arrived_ref, acts_ref, final_ref, picks_ref, routes_ref, w_ref, gain_ref, given_ref,
    normed_ref, dlogits_ref, out_ref, states_ref, weights_ref, rscale_ref,
):
    layers = picks_ref.shape[0]
    half = acts_ref.shape[2]

    @pl.when(zh_ref[0] == 0)
    def _():
        normed_ref[...] = given_ref[...]

    @pl.when(zh_ref[0] != 0)
    def _():
        refs = (picks_ref, routes_ref, w_ref, gain_ref)
        state = [arrived_ref[h] for h in range(HALVES)]
        for layer in range(layers):
            for h in range(HALVES):
                states_ref[layer, h] = state[h]
            state = forward_layer(layer, state, refs, normed_ref, weights_ref, rscale_ref)
        floats = [part.astype(F32) for part in state]
        total = sum(jnp.sum(part * part, axis=-1, keepdims=True) for part in floats)
        rscale = lax.rsqrt(total / (HALVES * half) + EPSILON)
        normal = [part * rscale for part in floats]
        varied = [acts_ref[h].astype(F32) * final_ref[h : h + 1, :] for h in range(HALVES)]
        mean = sum(jnp.sum(v * s, axis=-1, keepdims=True) for v, s in zip(varied, normal)) / (HALVES * half)
        back = [(rscale * (v - s * mean)).astype(BF16) for v, s in zip(varied, normal)]
        for layer in reversed(range(layers)):
            state = [states_ref[layer, h] for h in range(HALVES)]
            back = backward_layer(layer, back, state, refs, weights_ref, rscale_ref, dlogits_ref)
        for h in range(HALVES):
            out_ref[h] = back[h]


def last_kernel(
    zh_ref, arrived_ref, states_ref, weights_ref, rscale_ref, picks_ref, routes_ref, w_ref, gain_ref,
    given_ref, copies_ref, dlogits_ref,
):
    layers = picks_ref.shape[0]

    @pl.when(zh_ref[0] != 0)
    def _():
        dlogits_ref[...] = given_ref[...]

    @pl.when(zh_ref[0] == 0)
    def _():
        refs = (picks_ref, routes_ref, w_ref, gain_ref)
        back = [arrived_ref[h] for h in range(HALVES)]
        for layer in reversed(range(layers)):
            state = [states_ref[layer, h] for h in range(HALVES)]
            back = backward_layer(layer, back, state, refs, weights_ref, rscale_ref, dlogits_ref)

    for layer in range(layers):
        for group in range(copies_ref.shape[1]):
            copies_ref[layer, group] = dlogits_ref[layer]


def spread_kernel(normed_ref, order_ref, out_ref):
    layers, halves, tokens, half = normed_ref.shape
    rows = normed_ref[...].reshape(layers * halves * tokens, half)
    moved = jnp.dot(rows, order_ref[...], preferred_element_type=F32).astype(BF16)
    for layer in range(layers):
        for h in range(halves):
            at = (layer * halves + h) * tokens
            for group in range(out_ref.shape[1]):
                out_ref[layer, group, h] = moved[at : at + tokens, group * 128 : (group + 1) * 128]


def grad_kernel(normed_ref, dlogits_ref, out_ref):
    sources, halves, tokens, lanes = normed_ref.shape
    experts = dlogits_ref.shape[2]
    planes, rows = out_ref.shape[:2]
    dlogits = dlogits_ref[...].reshape(sources * tokens, experts)
    per_half = planes // halves
    for h in range(halves):
        normed = normed_ref[:, h].reshape(sources * tokens, lanes)
        term = lax.dot_general(normed, dlogits, (((0,), (0,)), ((), ())), preferred_element_type=F32)
        for plane in range(per_half):
            out_ref[h * per_half + plane] = term[plane * rows : (plane + 1) * rows]


def call(kernel, outs, args, scratch=(), scalars=1):
    smem = [pl.BlockSpec(memory_space=pltpu.SMEM)] * scalars
    vmem = pl.BlockSpec(memory_space=pltpu.VMEM)
    return pl.pallas_call(
        kernel,
        out_shape=outs,
        in_specs=smem + [vmem] * (len(args) - scalars),
        out_specs=jax.tree.map(lambda _: vmem, outs),
        scratch_shapes=list(scratch),
    )(*args)


def slot_numbers(routes):
    flattened = routes.reshape(routes.shape[0], -1)
    pair_count = flattened.shape[1]
    matches = flattened[:, :, None] == flattened[:, None, :]
    earlier = lax.broadcasted_iota(jnp.int32, (pair_count, pair_count), 1) < lax.broadcasted_iota(
        jnp.int32, (pair_count, pair_count), 0
    )
    return jnp.sum(jnp.where(matches & earlier[None], 1, 0), axis=-1).astype(jnp.int32).reshape(routes.shape)


def thirds(values):
    high = lax.reduce_precision(values, 8, 7)
    middle = lax.reduce_precision(values - high, 8, 7)
    return jnp.stack([high, middle, values - high - middle]).astype(BF16)


def from_all(shared, given, axis):
    count, here = lax.axis_size(axis), lax.axis_index(axis)
    slots = []
    for shift in range(count):
        mine = lax.dynamic_index_in_dim(given, (here + shift) % count, 0, keepdims=False)
        block = jnp.concatenate([shared, mine], axis=0)
        if shift:
            block = lax.ppermute(block, axis, [(source, (source + shift) % count) for source in range(count)])
        slots.append(block)
    slots = jnp.stack(slots)
    return jnp.concatenate(
        [lax.dynamic_slice_in_dim(slots, (here - source) % count, 1, 0) for source in range(count)]
    )


def compute(expert_axes, plane_axis, flat_axes, inputs, cotangent, expert_out, route_ids, router_w, norm_gain, final_gain):
    zh = lax.axis_index("zh")
    micros, tokens, part = inputs.shape
    layers = lax.axis_size("x")
    owners = lax.axis_size(expert_axes)
    local_experts, capacity, width = expert_out.shape[2], expert_out.shape[4], expert_out.shape[5]
    half = width // HALVES
    experts = router_w.shape[2]
    choices = route_ids.shape[3]
    zh_word = jnp.reshape(zh, (1,)).astype(jnp.int32)

    kept = jnp.where(zh == 0, inputs, cotangent)
    crossing = jnp.where(zh == 0, cotangent, inputs)
    crossed = lax.ppermute(crossing, "zh", [(0, 1), (1, 0)])

    rows = expert_out[0].reshape(micros, local_experts, owners, capacity, HALVES, half)
    rows = rows.transpose(0, 2, 1, 4, 3, 5).reshape(micros * owners, local_experts * HALVES * capacity, half)
    rows, router_here, gain_here, routes_here = lax.optimization_barrier(
        (rows, router_w[0], norm_gain[0], route_ids[0])
    )
    table = lax.all_to_all(rows, ("x",) + expert_axes, split_axis=0, concat_axis=0, tiled=True)
    table = table.reshape(layers, experts * HALVES * capacity, half)

    lower = jnp.where(zh == 0, kept, crossed)
    upper = jnp.where(zh == 0, crossed, kept)
    acts_part = jnp.stack([lower, upper], axis=2).reshape(micros, tokens * HALVES * part // 128, 128)
    act_rows = acts_part.shape[1]
    route_part = routes_here.astype(BF16).reshape(micros, tokens * choices // 128, 128)
    route_rows = route_part.shape[1]
    route_part = jnp.pad(route_part, ((0, 0), (0, 8 - route_rows), (0, 0)))
    gain_part = thirds(gain_here).reshape(3 * width // 128, 128)
    gain_rows = gain_part.shape[0]
    gain_part = jnp.pad(gain_part, ((0, -gain_rows % 8), (0, 0)))
    shared = jnp.concatenate([router_here, gain_part], axis=0)
    packed = from_all(shared, jnp.concatenate([acts_part, route_part], axis=1), "x")
    w_all = packed[:, :width]
    gain_all = packed[:, width : width + gain_rows].reshape(layers, 3, width).astype(F32)
    gain_all = (gain_all[:, 0] + gain_all[:, 1] + gain_all[:, 2]).reshape(layers, HALVES, half)
    at = shared.shape[0]
    acts = packed[:, at : at + act_rows].reshape(layers, tokens, HALVES, part)
    acts = acts.transpose(2, 1, 0, 3).reshape(HALVES, tokens, half)
    at += act_rows
    routes = packed[:, at : at + route_rows].reshape(layers, tokens, choices).astype(F32).astype(jnp.int32)

    target = routes * (HALVES * capacity) + slot_numbers(routes)
    target = target.transpose(0, 2, 1)[:, None] + (jnp.arange(HALVES) * capacity)[None, :, None, None]
    target = target.reshape(layers, HALVES * choices * tokens, 1)
    select = (target == jnp.arange(experts * HALVES * capacity)[None, None, :]).astype(BF16)

    planes = lax.axis_size(plane_axis)
    groups = owners // planes
    piece = width // owners
    feature = jnp.arange(half)
    place = feature // piece % groups * 128 + feature // (piece * groups) * piece + feature % piece
    order = (place[:, None] == jnp.arange(groups * 128)[None, :]).astype(BF16)

    shape = jax.ShapeDtypeStruct
    rows_shape = (HALVES, tokens, half)
    picks, states, normed, weights, rscale, sent = call(
        first_kernel,
        (
            shape((layers, HALVES, choices, tokens, half), BF16),
            shape((layers,) + rows_shape, BF16),
            shape((layers,) + rows_shape, BF16),
            shape((layers, choices, tokens, 128), F32),
            shape((layers, tokens, 128), F32),
            shape(rows_shape, BF16),
        ),
        (zh_word, table, select, routes, w_all, gain_all, acts),
    )
    arrived = lax.ppermute(sent, "zh", [(0, 1)])
    normed, dlogits, sent = call(
        middle_kernel,
        (
            shape((layers,) + rows_shape, BF16),
            shape((layers, tokens, experts), BF16),
            shape(rows_shape, BF16),
        ),
        (zh_word, arrived, acts, final_gain.reshape(HALVES, half), picks, routes, w_all, gain_all, normed),
        scratch=(
            pltpu.VMEM((layers,) + rows_shape, BF16),
            pltpu.VMEM((layers, choices, tokens, 128), F32),
            pltpu.VMEM((layers, tokens, 128), F32),
        ),
    )
    arrived = lax.ppermute(sent, "zh", [(1, 0)])
    normed = call(
        spread_kernel, shape((layers, groups, HALVES, tokens, 128), BF16), (normed, order), scalars=0
    )
    normed = normed.reshape(layers * groups, HALVES, tokens, 128)
    normed = lax.all_to_all(normed, ("x",) + flat_axes, split_axis=0, concat_axis=0, tiled=True)
    arrived, normed = lax.optimization_barrier((arrived, normed))
    dlogits, _ = call(
        last_kernel,
        (shape((layers, groups, tokens, experts), BF16), shape((layers, tokens, experts), BF16)),
        (zh_word, arrived, states, weights, rscale, picks, routes, w_all, gain_all, dlogits),
    )
    dlogits = dlogits.reshape(layers * groups, tokens, experts)
    dlogits = lax.all_to_all(dlogits, ("x",) + flat_axes, split_axis=0, concat_axis=0, tiled=True)
    term = call(grad_kernel, shape((planes, piece, experts), F32), (normed, dlogits), scalars=0)
    term = lax.all_to_all(term, plane_axis, split_axis=0, concat_axis=0, tiled=True)
    router_part = jnp.sum(term, axis=0)
    at = lax.axis_index(expert_axes) * (width // owners)
    w_slab = lax.dynamic_slice_in_dim(router_w[0], at, width // owners, 0).astype(F32)
    gain_slab = lax.dynamic_slice_in_dim(norm_gain[0], at, width // owners, 0)
    gain_part = jnp.sum(w_slab * router_part, axis=-1) / gain_slab
    return (router_part[None], gain_part[None])


def solution(mesh):
    sections, owners = mesh.shape["section"], mesh.shape["expert"]
    groups = 8
    planes = owners // groups
    wide = Mesh(mesh.devices.reshape(HALVES, sections // HALVES, planes, groups), ("zh", "x", "z", "yc"))
    section, expert = ("zh", "x"), ("z", "yc")
    placed = (
        P(None, expert, section),
        P(None, expert, section),
        P(section, None, expert, None, None, None),
        P(section, None, expert, None),
        P(section, None, None),
        P(section, None),
        P(),
    )
    return jax.shard_map(
        functools.partial(compute, expert, "z", ("yc",)),
        mesh=wide,
        in_specs=placed,
        out_specs=(P(section, expert, None), P(section, expert)),
        check_vma=False,
    )
```

```python
import functools

import jax
import jax.numpy as jnp
from jax import lax
from jax.experimental import pallas as pl
from jax.experimental.pallas import tpu as pltpu
from jax.sharding import Mesh, PartitionSpec as P


EPSILON = 1e-05
HALVES = 2
F32 = jnp.float32
BF16 = jnp.bfloat16


def onehots(routes_ref, layer, choices, experts):
    lanes = lax.broadcasted_iota(jnp.int32, (routes_ref.shape[1], experts), 1)
    rows = routes_ref[layer]
    return [rows[:, k : k + 1] == lanes for k in range(choices)]


def forward_layer(layer, state, refs, stats_ref, normed_ref=None):
    picks_ref, routes_ref, w_ref, gain_ref = refs
    tokens, half = state[0].shape
    experts = w_ref.shape[2]
    choices = routes_ref.shape[2]
    floats = [part.astype(F32) for part in state]
    total = sum(jnp.sum(part * part, axis=-1, keepdims=True) for part in floats)
    rscale = lax.rsqrt(total / (HALVES * half) + EPSILON)
    logits = jnp.zeros((tokens, experts), F32)
    for h in range(HALVES):
        normed = (floats[h] * rscale * gain_ref[layer, h : h + 1, :]).astype(BF16)
        if normed_ref is not None:
            normed_ref[layer, h] = normed
        logits += jnp.dot(normed, w_ref[layer, h * half : (h + 1) * half, :], preferred_element_type=F32)
    hots = onehots(routes_ref, layer, choices, experts)
    raised = [jnp.exp(jnp.sum(jnp.where(hot, logits, 0.0), axis=-1, keepdims=True)) for hot in hots]
    bottom = sum(raised)
    weights = [value / bottom for value in raised]
    lanes = lax.broadcasted_iota(jnp.int32, stats_ref.shape[1:], 1)
    stats = jnp.broadcast_to(rscale, lanes.shape)
    for k in range(choices):
        stats = jnp.where(lanes == k, weights[k], stats)
    stats_ref[layer] = stats
    fresh = []
    for h in range(HALVES):
        mixture = sum(weights[k] * picks_ref[layer, h, k].astype(F32) for k in range(choices))
        fresh.append((floats[h] + mixture).astype(BF16))
    return fresh


def backward_layer(layer, back, state, refs, stats_ref, dlogits_ref):
    picks_ref, routes_ref, w_ref, gain_ref = refs
    half = state[0].shape[1]
    experts = w_ref.shape[2]
    choices = routes_ref.shape[2]
    back_float = [part.astype(F32) for part in back]
    stats = stats_ref[layer]
    weights = [stats[:, k : k + 1] for k in range(choices)]
    rscale = stats[:, choices : choices + 1]
    dweights = [
        sum(
            jnp.sum(back_float[h] * picks_ref[layer, h, k].astype(F32), axis=-1, keepdims=True)
            for h in range(HALVES)
        )
        for k in range(choices)
    ]
    average = sum(w * d for w, d in zip(weights, dweights))
    dlogits = jnp.zeros((back[0].shape[0], experts), F32)
    for k, hot in enumerate(onehots(routes_ref, layer, choices, experts)):
        dlogits += jnp.where(hot, weights[k] * (dweights[k] - average), 0.0)
    dlogits = dlogits.astype(BF16)
    dlogits_ref[layer] = dlogits
    varied, normal = [], []
    for h in range(HALVES):
        dnormed = lax.dot_general(
            dlogits,
            w_ref[layer, h * half : (h + 1) * half, :],
            (((1,), (1,)), ((), ())),
            preferred_element_type=F32,
        )
        varied.append(dnormed * gain_ref[layer, h : h + 1, :])
        normal.append(state[h].astype(F32) * rscale)
    mean = sum(jnp.sum(v * s, axis=-1, keepdims=True) for v, s in zip(varied, normal)) / (HALVES * half)
    return [(b + rscale * (v - s * mean)).astype(BF16) for b, v, s in zip(back_float, varied, normal)]


def layout_kernel(rows_ref, out_ref, held_ref, stage_ref, in_sems, out_sems):
    micros, local_experts, owners, capacity, width = rows_ref.shape
    half = width // HALVES
    arriving = [
        [
            pltpu.make_async_copy(
                rows_ref.at[m, e], held_ref.at[m, e], in_sems.at[m * local_experts + e]
            )
            for e in range(local_experts)
        ]
        for m in range(micros)
    ]
    for copies in arriving:
        for copy in copies:
            copy.start()
    leaving = []
    for m in range(micros):
        blocks = pl.ds(m * owners, owners)
        for e in range(local_experts):
            arriving[m][e].wait()
            for h in range(HALVES):
                at = (e * HALVES + h) * capacity
                stage_ref[blocks, pl.ds(at, capacity), :] = held_ref[m, e, :, :, h * half : (h + 1) * half]
        leaving.append(pltpu.make_async_copy(stage_ref.at[blocks], out_ref.at[blocks], out_sems.at[m]))
        leaving[-1].start()
    for copy in leaving:
        copy.wait()


def pick_layer(layer, copies, table_ref, select_ref, picks_ref):
    tokens = picks_ref.shape[3]
    choices = picks_ref.shape[2]
    for copy in copies[layer]:
        copy.wait()
    rows = jnp.dot(select_ref[layer], table_ref[layer], preferred_element_type=F32).astype(BF16)
    for h in range(HALVES):
        for k in range(choices):
            at = (h * choices + k) * tokens
            picks_ref[layer, h, k] = rows[at : at + tokens]


def first_kernel(
    zh_ref, rows_ref, chosen_ref, routes_ref, w_ref, gain_ref, acts_ref,
    picks_ref, states_ref, stats_ref, out_ref, table_ref, select_ref, sems,
):
    layers = table_ref.shape[0]
    copies = [
        (
            pltpu.make_async_copy(chosen_ref.at[layer], select_ref.at[layer], sems.at[0, layer]),
            pltpu.make_async_copy(rows_ref.at[layer], table_ref.at[layer], sems.at[1, layer]),
        )
        for layer in range(layers)
    ]
    for pair in copies:
        for copy in pair:
            copy.start()

    @pl.when(zh_ref[0] != 0)
    def _():
        for layer in range(layers):
            pick_layer(layer, copies, table_ref, select_ref, picks_ref)

    @pl.when(zh_ref[0] == 0)
    def _():
        refs = (picks_ref, routes_ref, w_ref, gain_ref)
        state = [acts_ref[h] for h in range(HALVES)]
        for layer in range(layers):
            pick_layer(layer, copies, table_ref, select_ref, picks_ref)
            for h in range(HALVES):
                states_ref[layer, h] = state[h]
            state = forward_layer(layer, state, refs, stats_ref)
        for h in range(HALVES):
            out_ref[h] = state[h]


def middle_kernel(
    zh_ref, arrived_ref, acts_ref, final_ref, picks_ref, routes_ref, w_ref, gain_ref, given_states_ref, given_stats_ref,
    normed_ref, dlogits_ref, out_ref, states_ref, stats_ref,
):
    layers = picks_ref.shape[0]
    choices = routes_ref.shape[2]
    half = acts_ref.shape[2]

    @pl.when(zh_ref[0] == 0)
    def _():
        for layer in range(layers):
            rscale = given_stats_ref[layer][:, choices : choices + 1]
            for h in range(HALVES):
                floats = given_states_ref[layer, h].astype(F32)
                normed_ref[layer, h] = (floats * rscale * gain_ref[layer, h : h + 1, :]).astype(BF16)

    @pl.when(zh_ref[0] != 0)
    def _():
        refs = (picks_ref, routes_ref, w_ref, gain_ref)
        state = [arrived_ref[h] for h in range(HALVES)]
        for layer in range(layers):
            for h in range(HALVES):
                states_ref[layer, h] = state[h]
            state = forward_layer(layer, state, refs, stats_ref, normed_ref)
        floats = [part.astype(F32) for part in state]
        total = sum(jnp.sum(part * part, axis=-1, keepdims=True) for part in floats)
        rscale = lax.rsqrt(total / (HALVES * half) + EPSILON)
        normal = [part * rscale for part in floats]
        varied = [acts_ref[h].astype(F32) * final_ref[h : h + 1, :] for h in range(HALVES)]
        mean = sum(jnp.sum(v * s, axis=-1, keepdims=True) for v, s in zip(varied, normal)) / (HALVES * half)
        back = [(rscale * (v - s * mean)).astype(BF16) for v, s in zip(varied, normal)]
        for layer in reversed(range(layers)):
            state = [states_ref[layer, h] for h in range(HALVES)]
            back = backward_layer(layer, back, state, refs, stats_ref, dlogits_ref)
        for h in range(HALVES):
            out_ref[h] = back[h]


def last_kernel(
    zh_ref, arrived_ref, states_ref, stats_ref, picks_ref, routes_ref, w_ref, gain_ref, given_ref,
    copies_ref, dlogits_ref,
):
    layers = picks_ref.shape[0]

    @pl.when(zh_ref[0] != 0)
    def _():
        dlogits_ref[...] = given_ref[...]

    @pl.when(zh_ref[0] == 0)
    def _():
        refs = (picks_ref, routes_ref, w_ref, gain_ref)
        back = [arrived_ref[h] for h in range(HALVES)]
        for layer in reversed(range(layers)):
            state = [states_ref[layer, h] for h in range(HALVES)]
            back = backward_layer(layer, back, state, refs, stats_ref, dlogits_ref)

    for layer in range(layers):
        for group in range(copies_ref.shape[1]):
            copies_ref[layer, group] = dlogits_ref[layer]


def spread_kernel(normed_ref, order_ref, out_ref):
    layers, halves, tokens, half = normed_ref.shape
    rows = normed_ref[...].reshape(layers * halves * tokens, half)
    moved = jnp.dot(rows, order_ref[...], preferred_element_type=F32).astype(BF16)
    for layer in range(layers):
        for h in range(halves):
            at = (layer * halves + h) * tokens
            for group in range(out_ref.shape[1]):
                out_ref[layer, group, h] = moved[at : at + tokens, group * 128 : (group + 1) * 128]


def grad_kernel(normed_ref, dlogits_ref, out_ref):
    sources, halves, tokens, lanes = normed_ref.shape
    experts = dlogits_ref.shape[2]
    planes, rows = out_ref.shape[:2]
    dlogits = dlogits_ref[...].reshape(sources * tokens, experts)
    per_half = planes // halves
    for h in range(halves):
        normed = normed_ref[:, h].reshape(sources * tokens, lanes)
        term = lax.dot_general(normed, dlogits, (((0,), (0,)), ((), ())), preferred_element_type=F32)
        for plane in range(per_half):
            out_ref[h * per_half + plane] = term[plane * rows : (plane + 1) * rows]


def call(kernel, outs, args, scratch=(), scalars=1, apart=0, apart_out=False, limit=16):
    smem = [pl.BlockSpec(memory_space=pltpu.SMEM)] * scalars
    free = pl.BlockSpec(memory_space=pltpu.HBM)
    vmem = pl.BlockSpec(memory_space=pltpu.VMEM)
    far = [pltpu.with_memory_space_constraint(arg, pltpu.HBM) for arg in args[scalars : scalars + apart]]
    args = (*args[:scalars], *far, *args[scalars + apart :])
    return pl.pallas_call(
        kernel,
        out_shape=outs,
        in_specs=smem + [free] * apart + [vmem] * (len(args) - scalars - apart),
        out_specs=jax.tree.map(lambda _: free if apart_out else vmem, outs),
        scratch_shapes=list(scratch),
        compiler_params=pltpu.CompilerParams(vmem_limit_bytes=limit * 2**20),
    )(*args)


def slot_numbers(routes):
    flattened = routes.reshape(routes.shape[0], -1)
    pair_count = flattened.shape[1]
    matches = flattened[:, :, None] == flattened[:, None, :]
    earlier = lax.broadcasted_iota(jnp.int32, (pair_count, pair_count), 1) < lax.broadcasted_iota(
        jnp.int32, (pair_count, pair_count), 0
    )
    return jnp.sum(jnp.where(matches & earlier[None], 1, 0), axis=-1).astype(jnp.int32).reshape(routes.shape)


def thirds(values):
    high = lax.reduce_precision(values, 8, 7)
    middle = lax.reduce_precision(values - high, 8, 7)
    return jnp.stack([high, middle, values - high - middle]).astype(BF16)


def from_all(shared, given, axis):
    count, here = lax.axis_size(axis), lax.axis_index(axis)
    slots = []
    for shift in range(count):
        mine = lax.dynamic_index_in_dim(given, (here + shift) % count, 0, keepdims=False)
        block = jnp.concatenate([shared, mine], axis=0)
        if shift:
            block = lax.ppermute(block, axis, [(source, (source + shift) % count) for source in range(count)])
        slots.append(block)
    slots = jnp.stack(slots)
    return jnp.concatenate(
        [lax.dynamic_slice_in_dim(slots, (here - source) % count, 1, 0) for source in range(count)]
    )


def compute(expert_axes, plane_axis, flat_axes, inputs, cotangent, expert_out, route_ids, router_w, norm_gain, final_gain):
    zh = lax.axis_index("zh")
    micros, tokens, part = inputs.shape
    layers = lax.axis_size("x")
    owners = lax.axis_size(expert_axes)
    local_experts, capacity, width = expert_out.shape[2], expert_out.shape[4], expert_out.shape[5]
    half = width // HALVES
    experts = router_w.shape[2]
    choices = route_ids.shape[3]
    zh_word = jnp.reshape(zh, (1,)).astype(jnp.int32)

    kept = jnp.where(zh == 0, inputs, cotangent)
    crossing = jnp.where(zh == 0, cotangent, inputs)
    crossed = lax.ppermute(crossing, "zh", [(0, 1), (1, 0)])

    row_blocks = (micros * owners, local_experts * HALVES * capacity, half)
    rows = call(
        layout_kernel,
        jax.ShapeDtypeStruct(row_blocks, BF16),
        (expert_out[0],),
        scratch=(
            pltpu.VMEM(expert_out.shape[1:3] + expert_out.shape[3:], BF16),
            pltpu.VMEM(row_blocks, BF16),
            pltpu.SemaphoreType.DMA((micros * local_experts,)),
            pltpu.SemaphoreType.DMA((micros,)),
        ),
        scalars=0,
        apart=1,
        apart_out=True,
    )
    rows, router_here, gain_here, routes_here = lax.optimization_barrier(
        (rows, router_w[0], norm_gain[0], route_ids[0])
    )
    table = lax.all_to_all(rows, ("x",) + expert_axes, split_axis=0, concat_axis=0, tiled=True)
    table = table.reshape(layers, experts * HALVES * capacity, half)

    lower = jnp.where(zh == 0, kept, crossed)
    upper = jnp.where(zh == 0, crossed, kept)
    acts_part = jnp.stack([lower, upper], axis=2).reshape(micros, tokens * HALVES * part // 128, 128)
    act_rows = acts_part.shape[1]
    route_part = routes_here.astype(BF16).reshape(micros, tokens * choices // 128, 128)
    route_rows = route_part.shape[1]
    route_part = jnp.pad(route_part, ((0, 0), (0, 8 - route_rows), (0, 0)))
    gain_part = thirds(gain_here).reshape(3 * width // 128, 128)
    gain_rows = gain_part.shape[0]
    gain_part = jnp.pad(gain_part, ((0, -gain_rows % 8), (0, 0)))
    shared = jnp.concatenate([router_here, gain_part], axis=0)
    packed = from_all(shared, jnp.concatenate([acts_part, route_part], axis=1), "x")
    w_all = packed[:, :width]
    gain_all = packed[:, width : width + gain_rows].reshape(layers, 3, width).astype(F32)
    gain_all = (gain_all[:, 0] + gain_all[:, 1] + gain_all[:, 2]).reshape(layers, HALVES, half)
    at = shared.shape[0]
    acts = packed[:, at : at + act_rows].reshape(layers, tokens, HALVES, part)
    acts = acts.transpose(2, 1, 0, 3).reshape(HALVES, tokens, half)
    at += act_rows
    routes = packed[:, at : at + route_rows].reshape(layers, tokens, choices).astype(F32).astype(jnp.int32)

    target = routes * (HALVES * capacity) + slot_numbers(routes)
    target = target.transpose(0, 2, 1)[:, None] + (jnp.arange(HALVES) * capacity)[None, :, None, None]
    target = target.reshape(layers, HALVES * choices * tokens, 1)
    select = (target == jnp.arange(experts * HALVES * capacity)[None, None, :]).astype(BF16)

    planes = lax.axis_size(plane_axis)
    groups = owners // planes
    piece = width // owners
    feature = jnp.arange(half)
    place = feature // piece % groups * 128 + feature // (piece * groups) * piece + feature % piece
    order = (place[:, None] == jnp.arange(groups * 128)[None, :]).astype(BF16)

    shape = jax.ShapeDtypeStruct
    rows_shape = (HALVES, tokens, half)
    picks, states, stats, sent = call(
        first_kernel,
        (
            shape((layers, HALVES, choices, tokens, half), BF16),
            shape((layers,) + rows_shape, BF16),
            shape((layers, tokens, 128), F32),
            shape(rows_shape, BF16),
        ),
        (zh_word, table, select, routes, w_all, gain_all, acts),
        scratch=(
            pltpu.VMEM(table.shape, BF16),
            pltpu.VMEM(select.shape, BF16),
            pltpu.SemaphoreType.DMA((2, layers)),
        ),
        apart=2,
    )
    arrived = lax.ppermute(sent, "zh", [(0, 1)])
    normed, dlogits, sent = call(
        middle_kernel,
        (
            shape((layers,) + rows_shape, BF16),
            shape((layers, tokens, experts), BF16),
            shape(rows_shape, BF16),
        ),
        (
            zh_word, arrived, acts, final_gain.reshape(HALVES, half), picks, routes, w_all, gain_all, states, stats,
        ),
        scratch=(pltpu.VMEM((layers,) + rows_shape, BF16), pltpu.VMEM((layers, tokens, 128), F32)),
    )
    arrived = lax.ppermute(sent, "zh", [(1, 0)])
    normed = call(
        spread_kernel, shape((layers, groups, HALVES, tokens, 128), BF16), (normed, order), scalars=0
    )
    normed = normed.reshape(layers * groups, HALVES, tokens, 128)
    normed = lax.all_to_all(normed, ("x",) + flat_axes, split_axis=0, concat_axis=0, tiled=True)
    arrived, normed = lax.optimization_barrier((arrived, normed))
    dlogits = call(
        last_kernel,
        shape((layers, groups, tokens, experts), BF16),
        (zh_word, arrived, states, stats, picks, routes, w_all, gain_all, dlogits),
        scratch=(pltpu.VMEM((layers, tokens, experts), BF16),),
    )
    dlogits = dlogits.reshape(layers * groups, tokens, experts)
    dlogits = lax.all_to_all(dlogits, ("x",) + flat_axes, split_axis=0, concat_axis=0, tiled=True)
    term = call(grad_kernel, shape((planes, piece, experts), F32), (normed, dlogits), scalars=0)
    term = lax.all_to_all(term, plane_axis, split_axis=0, concat_axis=0, tiled=True)
    router_part = jnp.sum(term, axis=0)
    at = lax.axis_index(expert_axes) * (width // owners)
    w_slab = lax.dynamic_slice_in_dim(router_w[0], at, width // owners, 0).astype(F32)
    gain_slab = lax.dynamic_slice_in_dim(norm_gain[0], at, width // owners, 0)
    gain_part = jnp.sum(w_slab * router_part, axis=-1) / gain_slab
    return (router_part[None], gain_part[None])


def solution(mesh):
    sections, owners = mesh.shape["section"], mesh.shape["expert"]
    groups = 8
    planes = owners // groups
    wide = Mesh(mesh.devices.reshape(HALVES, sections // HALVES, planes, groups), ("zh", "x", "z", "yc"))
    section, expert = ("zh", "x"), ("z", "yc")
    placed = (
        P(None, expert, section),
        P(None, expert, section),
        P(section, None, expert, None, None, None),
        P(section, None, expert, None),
        P(section, None, None),
        P(section, None),
        P(),
    )
    return jax.shard_map(
        functools.partial(compute, expert, "z", ("yc",)),
        mesh=wide,
        in_specs=placed,
        out_specs=(P(section, expert, None), P(section, expert)),
        check_vma=False,
    )
```

```python
import functools

import jax
import jax.numpy as jnp
from jax import lax
from jax.experimental import pallas as pl
from jax.experimental.pallas import tpu as pltpu
from jax.sharding import Mesh, PartitionSpec as P


EPSILON = 1e-05
HALVES = 2
F32 = jnp.float32
BF16 = jnp.bfloat16


def onehots(routes_ref, layer, choices, experts):
    lanes = lax.broadcasted_iota(jnp.int32, (routes_ref.shape[1], experts), 1)
    rows = routes_ref[layer]
    return [rows[:, k : k + 1] == lanes for k in range(choices)]


def forward_layer(layer, state, refs, stats_ref, normed_ref=None):
    picks_ref, routes_ref, w_ref, gain_ref = refs
    tokens, half = state[0].shape
    experts = w_ref.shape[2]
    choices = routes_ref.shape[2]
    floats = [part.astype(F32) for part in state]
    total = sum(jnp.sum(part * part, axis=-1, keepdims=True) for part in floats)
    rscale = lax.rsqrt(total / (HALVES * half) + EPSILON)
    logits = jnp.zeros((tokens, experts), F32)
    for h in range(HALVES):
        normed = (floats[h] * rscale * gain_ref[layer, h : h + 1, :]).astype(BF16)
        if normed_ref is not None:
            normed_ref[layer, h] = normed
        logits += jnp.dot(normed, w_ref[layer, h * half : (h + 1) * half, :], preferred_element_type=F32)
    hots = onehots(routes_ref, layer, choices, experts)
    raised = [jnp.exp(jnp.sum(jnp.where(hot, logits, 0.0), axis=-1, keepdims=True)) for hot in hots]
    bottom = sum(raised)
    weights = [value / bottom for value in raised]
    lanes = lax.broadcasted_iota(jnp.int32, stats_ref.shape[1:], 1)
    stats = jnp.broadcast_to(rscale, lanes.shape)
    for k in range(choices):
        stats = jnp.where(lanes == k, weights[k], stats)
    stats_ref[layer] = stats
    fresh = []
    for h in range(HALVES):
        mixture = sum(weights[k] * picks_ref[layer, h, k].astype(F32) for k in range(choices))
        fresh.append((floats[h] + mixture).astype(BF16))
    return fresh


def backward_layer(layer, back, state, refs, stats_ref, dlogits_ref):
    picks_ref, routes_ref, w_ref, gain_ref = refs
    half = state[0].shape[1]
    experts = w_ref.shape[2]
    choices = routes_ref.shape[2]
    back_float = [part.astype(F32) for part in back]
    stats = stats_ref[layer]
    weights = [stats[:, k : k + 1] for k in range(choices)]
    rscale = stats[:, choices : choices + 1]
    dweights = [
        sum(
            jnp.sum(back_float[h] * picks_ref[layer, h, k].astype(F32), axis=-1, keepdims=True)
            for h in range(HALVES)
        )
        for k in range(choices)
    ]
    average = sum(w * d for w, d in zip(weights, dweights))
    dlogits = jnp.zeros((back[0].shape[0], experts), F32)
    for k, hot in enumerate(onehots(routes_ref, layer, choices, experts)):
        dlogits += jnp.where(hot, weights[k] * (dweights[k] - average), 0.0)
    dlogits = dlogits.astype(BF16)
    dlogits_ref[layer] = dlogits
    varied, normal = [], []
    for h in range(HALVES):
        dnormed = lax.dot_general(
            dlogits,
            w_ref[layer, h * half : (h + 1) * half, :],
            (((1,), (1,)), ((), ())),
            preferred_element_type=F32,
        )
        varied.append(dnormed * gain_ref[layer, h : h + 1, :])
        normal.append(state[h].astype(F32) * rscale)
    mean = sum(jnp.sum(v * s, axis=-1, keepdims=True) for v, s in zip(varied, normal)) / (HALVES * half)
    return [(b + rscale * (v - s * mean)).astype(BF16) for b, v, s in zip(back_float, varied, normal)]


def layout_kernel(planes, zh_ref, rows_ref, out_ref, held_ref, stage_ref, in_sems, out_sems):
    micros, local_experts, owners, capacity, width = rows_ref.shape
    half = width // HALVES
    group = owners // planes
    arriving = [
        [
            pltpu.make_async_copy(
                rows_ref.at[m, e], held_ref.at[m, e], in_sems.at[m * local_experts + e]
            )
            for e in range(local_experts)
        ]
        for m in range(micros)
    ]
    for copies in arriving:
        for copy in copies:
            copy.start()
    leaving = []
    for m in range(micros):
        for e in range(local_experts):
            arriving[m][e].wait()
            for h in range(HALVES):
                at = (e * HALVES + h) * capacity
                stage_ref[pl.ds(m * owners, owners), pl.ds(at, capacity), :] = held_ref[
                    m, e, :, :, h * half : (h + 1) * half
                ]
        for plane in range(planes):
            site = jnp.where(zh_ref[0] == 0, plane, plane ^ 1)
            leaving.append(
                pltpu.make_async_copy(
                    stage_ref.at[pl.ds(m * owners + plane * group, group)],
                    out_ref.at[pl.ds(m * owners + site * group, group)],
                    out_sems.at[m * planes + plane],
                )
            )
            leaving[-1].start()
    for copy in leaving:
        copy.wait()


def pick_layer(layer, copies, table_ref, select_ref, picks_ref):
    tokens = picks_ref.shape[3]
    choices = picks_ref.shape[2]
    for copy in copies[layer]:
        copy.wait()
    rows = jnp.dot(select_ref[layer], table_ref[layer], preferred_element_type=F32).astype(BF16)
    for h in range(HALVES):
        for k in range(choices):
            at = (h * choices + k) * tokens
            picks_ref[layer, h, k] = rows[at : at + tokens]


def first_kernel(
    zh_ref, rows_ref, chosen_ref, routes_ref, w_ref, gain_ref, acts_ref,
    picks_ref, states_ref, stats_ref, out_ref, table_ref, select_ref, sems,
):
    layers = table_ref.shape[0]
    copies = [
        (
            pltpu.make_async_copy(chosen_ref.at[layer], select_ref.at[layer], sems.at[0, layer]),
            pltpu.make_async_copy(rows_ref.at[layer], table_ref.at[layer], sems.at[1, layer]),
        )
        for layer in range(layers)
    ]
    for pair in copies:
        for copy in pair:
            copy.start()

    @pl.when(zh_ref[0] != 0)
    def _():
        for layer in range(layers):
            pick_layer(layer, copies, table_ref, select_ref, picks_ref)

    @pl.when(zh_ref[0] == 0)
    def _():
        refs = (picks_ref, routes_ref, w_ref, gain_ref)
        state = [acts_ref[h] for h in range(HALVES)]
        for layer in range(layers):
            pick_layer(layer, copies, table_ref, select_ref, picks_ref)
            for h in range(HALVES):
                states_ref[layer, h] = state[h]
            state = forward_layer(layer, state, refs, stats_ref)
        for h in range(HALVES):
            out_ref[h] = state[h]


def middle_kernel(
    zh_ref, arrived_ref, acts_ref, final_ref, picks_ref, routes_ref, w_ref, gain_ref, given_states_ref, given_stats_ref,
    normed_ref, dlogits_ref, out_ref, states_ref, stats_ref,
):
    layers = picks_ref.shape[0]
    choices = routes_ref.shape[2]
    half = acts_ref.shape[2]

    @pl.when(zh_ref[0] == 0)
    def _():
        for layer in range(layers):
            rscale = given_stats_ref[layer][:, choices : choices + 1]
            for h in range(HALVES):
                floats = given_states_ref[layer, h].astype(F32)
                normed_ref[layer, h] = (floats * rscale * gain_ref[layer, h : h + 1, :]).astype(BF16)

    @pl.when(zh_ref[0] != 0)
    def _():
        refs = (picks_ref, routes_ref, w_ref, gain_ref)
        state = [arrived_ref[h] for h in range(HALVES)]
        for layer in range(layers):
            for h in range(HALVES):
                states_ref[layer, h] = state[h]
            state = forward_layer(layer, state, refs, stats_ref, normed_ref)
        floats = [part.astype(F32) for part in state]
        total = sum(jnp.sum(part * part, axis=-1, keepdims=True) for part in floats)
        rscale = lax.rsqrt(total / (HALVES * half) + EPSILON)
        normal = [part * rscale for part in floats]
        varied = [acts_ref[h].astype(F32) * final_ref[h : h + 1, :] for h in range(HALVES)]
        mean = sum(jnp.sum(v * s, axis=-1, keepdims=True) for v, s in zip(varied, normal)) / (HALVES * half)
        back = [(rscale * (v - s * mean)).astype(BF16) for v, s in zip(varied, normal)]
        for layer in reversed(range(layers)):
            state = [states_ref[layer, h] for h in range(HALVES)]
            back = backward_layer(layer, back, state, refs, stats_ref, dlogits_ref)
        for h in range(HALVES):
            out_ref[h] = back[h]


def last_kernel(
    zh_ref, arrived_ref, states_ref, stats_ref, picks_ref, routes_ref, w_ref, gain_ref, given_ref,
    copies_ref, dlogits_ref,
):
    layers = picks_ref.shape[0]

    @pl.when(zh_ref[0] != 0)
    def _():
        dlogits_ref[...] = given_ref[...]

    @pl.when(zh_ref[0] == 0)
    def _():
        refs = (picks_ref, routes_ref, w_ref, gain_ref)
        back = [arrived_ref[h] for h in range(HALVES)]
        for layer in reversed(range(layers)):
            state = [states_ref[layer, h] for h in range(HALVES)]
            back = backward_layer(layer, back, state, refs, stats_ref, dlogits_ref)

    for layer in range(layers):
        for group in range(copies_ref.shape[1]):
            copies_ref[layer, group] = dlogits_ref[layer]


def spread_kernel(normed_ref, order_ref, out_ref):
    layers, halves, tokens, half = normed_ref.shape
    rows = normed_ref[...].reshape(layers * halves * tokens, half)
    moved = jnp.dot(rows, order_ref[...], preferred_element_type=F32).astype(BF16)
    for layer in range(layers):
        for h in range(halves):
            at = (layer * halves + h) * tokens
            for group in range(out_ref.shape[1]):
                out_ref[layer, group, h] = moved[at : at + tokens, group * 128 : (group + 1) * 128]


def grad_kernel(normed_ref, dlogits_ref, out_ref):
    sources, halves, tokens, lanes = normed_ref.shape
    experts = dlogits_ref.shape[2]
    planes, rows = out_ref.shape[:2]
    dlogits = dlogits_ref[...].reshape(sources * tokens, experts)
    per_half = planes // halves
    for h in range(halves):
        normed = normed_ref[:, h].reshape(sources * tokens, lanes)
        term = lax.dot_general(normed, dlogits, (((0,), (0,)), ((), ())), preferred_element_type=F32)
        for plane in range(per_half):
            out_ref[h * per_half + plane] = term[plane * rows : (plane + 1) * rows].astype(BF16)


def call(kernel, outs, args, scratch=(), scalars=1, apart=0, apart_out=False, limit=16):
    smem = [pl.BlockSpec(memory_space=pltpu.SMEM)] * scalars
    free = pl.BlockSpec(memory_space=pltpu.HBM)
    vmem = pl.BlockSpec(memory_space=pltpu.VMEM)
    far = [pltpu.with_memory_space_constraint(arg, pltpu.HBM) for arg in args[scalars : scalars + apart]]
    args = (*args[:scalars], *far, *args[scalars + apart :])
    return pl.pallas_call(
        kernel,
        out_shape=outs,
        in_specs=smem + [free] * apart + [vmem] * (len(args) - scalars - apart),
        out_specs=jax.tree.map(lambda _: free if apart_out else vmem, outs),
        scratch_shapes=list(scratch),
        compiler_params=pltpu.CompilerParams(vmem_limit_bytes=limit * 2**20),
    )(*args)


def slot_numbers(routes):
    flattened = routes.reshape(routes.shape[0], -1)
    pair_count = flattened.shape[1]
    matches = flattened[:, :, None] == flattened[:, None, :]
    earlier = lax.broadcasted_iota(jnp.int32, (pair_count, pair_count), 1) < lax.broadcasted_iota(
        jnp.int32, (pair_count, pair_count), 0
    )
    return jnp.sum(jnp.where(matches & earlier[None], 1, 0), axis=-1).astype(jnp.int32).reshape(routes.shape)


def thirds(values):
    high = lax.reduce_precision(values, 8, 7)
    middle = lax.reduce_precision(values - high, 8, 7)
    return jnp.stack([high, middle, values - high - middle]).astype(BF16)


def from_all(rows, axis, addressed=False):
    count, here = lax.axis_size(axis), lax.axis_index(axis)
    slots = []
    for shift in range(count):
        block = lax.dynamic_index_in_dim(rows, (here + shift) % count, 0, keepdims=False) if addressed else rows
        if shift:
            block = lax.ppermute(block, axis, [(source, (source + shift) % count) for source in range(count)])
        slots.append(block)
    slots = jnp.stack(slots)
    return jnp.concatenate(
        [lax.dynamic_slice_in_dim(slots, (here - source) % count, 1, 0) for source in range(count)]
    )


def compute(expert_axes, plane_axis, flat_axes, inputs, cotangent, expert_out, route_ids, router_w, norm_gain, final_gain):
    zh = lax.axis_index("zh")
    micros, tokens, part = inputs.shape
    layers = lax.axis_size("x")
    owners = lax.axis_size(expert_axes)
    local_experts, capacity, width = expert_out.shape[2], expert_out.shape[4], expert_out.shape[5]
    half = width // HALVES
    experts = router_w.shape[2]
    choices = route_ids.shape[3]
    zh_word = jnp.reshape(zh, (1,)).astype(jnp.int32)

    kept = jnp.where(zh == 0, inputs, cotangent)
    crossing = jnp.where(zh == 0, cotangent, inputs)
    planes = lax.axis_size(plane_axis)
    lines = ("zh", plane_axis)
    there = [(plane, planes + (plane ^ 1)) for plane in range(planes)]
    crossed = lax.ppermute(crossing, lines, there + [(planes + plane, plane) for plane in range(planes)])

    row_blocks = (micros * owners, local_experts * HALVES * capacity, half)
    rows = call(
        functools.partial(layout_kernel, planes),
        jax.ShapeDtypeStruct(row_blocks, BF16),
        (zh_word, expert_out[0]),
        scratch=(
            pltpu.VMEM(expert_out.shape[1:3] + expert_out.shape[3:], BF16),
            pltpu.VMEM(row_blocks, BF16),
            pltpu.SemaphoreType.DMA((micros * local_experts,)),
            pltpu.SemaphoreType.DMA((micros * planes,)),
        ),
        apart=1,
        apart_out=True,
    )
    rows, router_here, gain_here, routes_here = lax.optimization_barrier(
        (rows, router_w[0], norm_gain[0], route_ids[0])
    )
    table = lax.all_to_all(rows, ("x",) + expert_axes, split_axis=0, concat_axis=0, tiled=True)
    table = table.reshape(layers, experts * HALVES * capacity, half)

    route_part = routes_here.astype(BF16).reshape(micros, tokens * choices // 128, 128)
    route_rows = route_part.shape[1]
    route_part = jnp.pad(route_part, ((0, 0), (0, 8 - route_rows), (0, 0)))
    act_rows = tokens * part // 128
    held = jnp.concatenate([kept.reshape(micros, act_rows, 128), route_part], axis=1)
    swapped = lax.ppermute(held, lines, [(planes + plane, planes + (plane ^ 1)) for plane in range(planes)])
    held = jnp.where(zh == 0, held, swapped)
    crossed = crossed.reshape(micros, act_rows, 128)
    lower = jnp.where(zh == 0, held[:, :act_rows], crossed)
    upper = jnp.where(zh == 0, crossed, held[:, :act_rows])
    given = jnp.concatenate([lower, upper, held[:, act_rows:]], axis=1)
    gain_part = thirds(gain_here).reshape(3 * width // 128, 128)
    gain_rows = gain_part.shape[0]
    gain_part = jnp.pad(gain_part, ((0, -gain_rows % 8), (0, 0)))
    shared = jnp.concatenate([router_here, gain_part], axis=0)
    packed = from_all(shared, "x")
    w_all = packed[:, :width]
    gain_all = packed[:, width : width + gain_rows].reshape(layers, 3, width).astype(F32)
    gain_all = (gain_all[:, 0] + gain_all[:, 1] + gain_all[:, 2]).reshape(layers, HALVES, half)
    packed = from_all(given, "x", True)
    acts = packed[:, : HALVES * act_rows].reshape(layers, HALVES, tokens, part)
    acts = acts.transpose(1, 2, 0, 3).reshape(HALVES, tokens, half)
    at = HALVES * act_rows
    routes = packed[:, at : at + route_rows].reshape(layers, tokens, choices).astype(F32).astype(jnp.int32)

    target = routes * (HALVES * capacity) + slot_numbers(routes)
    target = target.transpose(0, 2, 1)[:, None] + (jnp.arange(HALVES) * capacity)[None, :, None, None]
    target = target.reshape(layers, HALVES * choices * tokens, 1)
    select = (target == jnp.arange(experts * HALVES * capacity)[None, None, :]).astype(BF16)

    groups = owners // planes
    piece = width // owners
    feature = jnp.arange(half)
    place = feature // piece % groups * 128 + feature // (piece * groups) * piece + feature % piece
    order = (place[:, None] == jnp.arange(groups * 128)[None, :]).astype(BF16)

    shape = jax.ShapeDtypeStruct
    rows_shape = (HALVES, tokens, half)
    picks, states, stats, sent = call(
        first_kernel,
        (
            shape((layers, HALVES, choices, tokens, half), BF16),
            shape((layers,) + rows_shape, BF16),
            shape((layers, tokens, 128), F32),
            shape(rows_shape, BF16),
        ),
        (zh_word, table, select, routes, w_all, gain_all, acts),
        scratch=(
            pltpu.VMEM(table.shape, BF16),
            pltpu.VMEM(select.shape, BF16),
            pltpu.SemaphoreType.DMA((2, layers)),
        ),
        apart=2,
    )
    arrived = lax.ppermute(sent, lines, there)
    normed, dlogits, sent = call(
        middle_kernel,
        (
            shape((layers,) + rows_shape, BF16),
            shape((layers, tokens, experts), BF16),
            shape(rows_shape, BF16),
        ),
        (
            zh_word, arrived, acts, final_gain.reshape(HALVES, half), picks, routes, w_all, gain_all, states, stats,
        ),
        scratch=(pltpu.VMEM((layers,) + rows_shape, BF16), pltpu.VMEM((layers, tokens, 128), F32)),
    )
    arrived = lax.ppermute(sent, lines, [(target, source) for source, target in there])
    normed = call(
        spread_kernel, shape((layers, groups, HALVES, tokens, 128), BF16), (normed, order), scalars=0
    )
    normed = normed.reshape(layers * groups, HALVES, tokens, 128)
    normed = lax.all_to_all(normed, ("x",) + flat_axes, split_axis=0, concat_axis=0, tiled=True)
    arrived, normed = lax.optimization_barrier((arrived, normed))
    dlogits = call(
        last_kernel,
        shape((layers, groups, tokens, experts), BF16),
        (zh_word, arrived, states, stats, picks, routes, w_all, gain_all, dlogits),
        scratch=(pltpu.VMEM((layers, tokens, experts), BF16),),
    )
    dlogits = dlogits.reshape(layers * groups, tokens, experts)
    dlogits = lax.all_to_all(dlogits, ("x",) + flat_axes, split_axis=0, concat_axis=0, tiled=True)
    term = call(grad_kernel, shape((planes, piece, experts), BF16), (normed, dlogits), scalars=0)
    term = lax.all_to_all(term, plane_axis, split_axis=0, concat_axis=0, tiled=True)
    router_part = jnp.sum(term.astype(F32), axis=0)
    at = lax.axis_index(expert_axes) * (width // owners)
    w_slab = lax.dynamic_slice_in_dim(router_w[0], at, width // owners, 0).astype(F32)
    gain_slab = lax.dynamic_slice_in_dim(norm_gain[0], at, width // owners, 0)
    gain_part = jnp.sum(w_slab * router_part, axis=-1) / gain_slab
    return (router_part[None], gain_part[None])


def solution(mesh):
    sections, owners = mesh.shape["section"], mesh.shape["expert"]
    groups = 8
    planes = owners // groups
    wide = Mesh(mesh.devices.reshape(HALVES, sections // HALVES, planes, groups), ("zh", "x", "z", "yc"))
    section, expert = ("zh", "x"), ("z", "yc")
    placed = (
        P(None, expert, section),
        P(None, expert, section),
        P(section, None, expert, None, None, None),
        P(section, None, expert, None),
        P(section, None, None),
        P(section, None),
        P(),
    )
    return jax.shard_map(
        functools.partial(compute, expert, "z", ("yc",)),
        mesh=wide,
        in_specs=placed,
        out_specs=(P(section, expert, None), P(section, expert)),
        check_vma=False,
    )
```

```python
import functools

import jax
import jax.numpy as jnp
from jax import lax
from jax.experimental import pallas as pl
from jax.experimental.pallas import tpu as pltpu
from jax.sharding import Mesh, PartitionSpec as P


EPSILON = 1e-05
HALVES = 2
F32 = jnp.float32
BF16 = jnp.bfloat16


def onehots(routes_ref, layer, choices, experts):
    lanes = lax.broadcasted_iota(jnp.int32, (routes_ref.shape[1], experts), 1)
    rows = routes_ref[layer]
    return [rows[:, k : k + 1] == lanes for k in range(choices)]


def forward_layer(layer, state, refs, stats_ref, normed_ref=None):
    picks_ref, routes_ref, w_ref, gain_ref = refs
    tokens, half = state[0].shape
    experts = w_ref.shape[2]
    choices = routes_ref.shape[2]
    floats = [part.astype(F32) for part in state]
    total = sum(jnp.sum(part * part, axis=-1, keepdims=True) for part in floats)
    rscale = lax.rsqrt(total / (HALVES * half) + EPSILON)
    logits = jnp.zeros((tokens, experts), F32)
    for h in range(HALVES):
        normed = (floats[h] * rscale * gain_ref[layer, h : h + 1, :]).astype(BF16)
        if normed_ref is not None:
            normed_ref[layer, h] = normed
        logits += jnp.dot(normed, w_ref[layer, h * half : (h + 1) * half, :], preferred_element_type=F32)
    hots = onehots(routes_ref, layer, choices, experts)
    raised = [jnp.exp(jnp.sum(jnp.where(hot, logits, 0.0), axis=-1, keepdims=True)) for hot in hots]
    bottom = sum(raised)
    weights = [value / bottom for value in raised]
    lanes = lax.broadcasted_iota(jnp.int32, stats_ref.shape[1:], 1)
    stats = jnp.broadcast_to(rscale, lanes.shape)
    for k in range(choices):
        stats = jnp.where(lanes == k, weights[k], stats)
    stats_ref[layer] = stats
    fresh = []
    for h in range(HALVES):
        mixture = sum(weights[k] * picks_ref[layer, h, k].astype(F32) for k in range(choices))
        fresh.append((floats[h] + mixture).astype(BF16))
    return fresh


def backward_layer(layer, back, state, refs, stats_ref, dlogits_ref):
    picks_ref, routes_ref, w_ref, gain_ref = refs
    half = state[0].shape[1]
    experts = w_ref.shape[2]
    choices = routes_ref.shape[2]
    back_float = [part.astype(F32) for part in back]
    stats = stats_ref[layer]
    weights = [stats[:, k : k + 1] for k in range(choices)]
    rscale = stats[:, choices : choices + 1]
    dweights = [
        sum(
            jnp.sum(back_float[h] * picks_ref[layer, h, k].astype(F32), axis=-1, keepdims=True)
            for h in range(HALVES)
        )
        for k in range(choices)
    ]
    average = sum(w * d for w, d in zip(weights, dweights))
    dlogits = jnp.zeros((back[0].shape[0], experts), F32)
    for k, hot in enumerate(onehots(routes_ref, layer, choices, experts)):
        dlogits += jnp.where(hot, weights[k] * (dweights[k] - average), 0.0)
    dlogits = dlogits.astype(BF16)
    dlogits_ref[layer] = dlogits
    varied, normal = [], []
    for h in range(HALVES):
        dnormed = lax.dot_general(
            dlogits,
            w_ref[layer, h * half : (h + 1) * half, :],
            (((1,), (1,)), ((), ())),
            preferred_element_type=F32,
        )
        varied.append(dnormed * gain_ref[layer, h : h + 1, :])
        normal.append(state[h].astype(F32) * rscale)
    mean = sum(jnp.sum(v * s, axis=-1, keepdims=True) for v, s in zip(varied, normal)) / (HALVES * half)
    return [(b + rscale * (v - s * mean)).astype(BF16) for b, v, s in zip(back_float, varied, normal)]


def layout_kernel(planes, zh_ref, rows_ref, out_ref, held_ref, stage_ref, in_sems, out_sems):
    micros, local_experts, owners, capacity, width = rows_ref.shape
    half = width // HALVES
    group = owners // planes
    arriving = [
        [
            pltpu.make_async_copy(
                rows_ref.at[m, e], held_ref.at[m, e], in_sems.at[m * local_experts + e]
            )
            for e in range(local_experts)
        ]
        for m in range(micros)
    ]
    for copies in arriving:
        for copy in copies:
            copy.start()
    leaving = []
    for m in range(micros):
        for e in range(local_experts):
            arriving[m][e].wait()
            for h in range(HALVES):
                at = (e * HALVES + h) * capacity
                stage_ref[pl.ds(m * owners, owners), pl.ds(at, capacity), :] = held_ref[
                    m, e, :, :, h * half : (h + 1) * half
                ]
        for plane in range(planes):
            site = jnp.where(zh_ref[0] == 0, plane, plane ^ 1)
            leaving.append(
                pltpu.make_async_copy(
                    stage_ref.at[pl.ds(m * owners + plane * group, group)],
                    out_ref.at[pl.ds(m * owners + site * group, group)],
                    out_sems.at[m * planes + plane],
                )
            )
            leaving[-1].start()
    for copy in leaving:
        copy.wait()


def pick_layer(layer, copies, table_ref, select_ref, picks_ref):
    tokens = picks_ref.shape[3]
    choices = picks_ref.shape[2]
    for copy in copies[layer]:
        copy.wait()
    rows = jnp.dot(select_ref[layer], table_ref[layer], preferred_element_type=F32).astype(BF16)
    for h in range(HALVES):
        for k in range(choices):
            at = (h * choices + k) * tokens
            picks_ref[layer, h, k] = rows[at : at + tokens]


def first_kernel(
    zh_ref, rows_ref, chosen_ref, routes_ref, w_ref, gain_ref, acts_ref,
    picks_ref, states_ref, stats_ref, out_ref, table_ref, select_ref, sems,
):
    layers = table_ref.shape[0]
    copies = [
        (
            pltpu.make_async_copy(chosen_ref.at[layer], select_ref.at[layer], sems.at[0, layer]),
            pltpu.make_async_copy(rows_ref.at[layer], table_ref.at[layer], sems.at[1, layer]),
        )
        for layer in range(layers)
    ]
    for pair in copies:
        for copy in pair:
            copy.start()

    @pl.when(zh_ref[0] != 0)
    def _():
        for layer in range(layers):
            pick_layer(layer, copies, table_ref, select_ref, picks_ref)

    @pl.when(zh_ref[0] == 0)
    def _():
        refs = (picks_ref, routes_ref, w_ref, gain_ref)
        state = [acts_ref[h] for h in range(HALVES)]
        for layer in range(layers):
            pick_layer(layer, copies, table_ref, select_ref, picks_ref)
            for h in range(HALVES):
                states_ref[layer, h] = state[h]
            state = forward_layer(layer, state, refs, stats_ref)
        for h in range(HALVES):
            out_ref[h] = state[h]


def middle_kernel(
    zh_ref, arrived_ref, acts_ref, final_ref, picks_ref, routes_ref, w_ref, gain_ref, given_states_ref, given_stats_ref,
    normed_ref, dlogits_ref, out_ref, states_ref, stats_ref,
):
    layers = picks_ref.shape[0]
    choices = routes_ref.shape[2]
    half = acts_ref.shape[2]

    @pl.when(zh_ref[0] == 0)
    def _():
        for layer in range(layers):
            rscale = given_stats_ref[layer][:, choices : choices + 1]
            for h in range(HALVES):
                floats = given_states_ref[layer, h].astype(F32)
                normed_ref[layer, h] = (floats * rscale * gain_ref[layer, h : h + 1, :]).astype(BF16)

    @pl.when(zh_ref[0] != 0)
    def _():
        refs = (picks_ref, routes_ref, w_ref, gain_ref)
        state = [arrived_ref[h] for h in range(HALVES)]
        for layer in range(layers):
            for h in range(HALVES):
                states_ref[layer, h] = state[h]
            state = forward_layer(layer, state, refs, stats_ref, normed_ref)
        floats = [part.astype(F32) for part in state]
        total = sum(jnp.sum(part * part, axis=-1, keepdims=True) for part in floats)
        rscale = lax.rsqrt(total / (HALVES * half) + EPSILON)
        normal = [part * rscale for part in floats]
        varied = [acts_ref[h].astype(F32) * final_ref[h : h + 1, :] for h in range(HALVES)]
        mean = sum(jnp.sum(v * s, axis=-1, keepdims=True) for v, s in zip(varied, normal)) / (HALVES * half)
        back = [(rscale * (v - s * mean)).astype(BF16) for v, s in zip(varied, normal)]
        for layer in reversed(range(layers)):
            state = [states_ref[layer, h] for h in range(HALVES)]
            back = backward_layer(layer, back, state, refs, stats_ref, dlogits_ref)
        for h in range(HALVES):
            out_ref[h] = back[h]


def last_kernel(
    zh_ref, arrived_ref, states_ref, stats_ref, picks_ref, routes_ref, w_ref, gain_ref, given_ref,
    copies_ref, dlogits_ref,
):
    layers = picks_ref.shape[0]

    @pl.when(zh_ref[0] != 0)
    def _():
        dlogits_ref[...] = given_ref[...]

    @pl.when(zh_ref[0] == 0)
    def _():
        refs = (picks_ref, routes_ref, w_ref, gain_ref)
        back = [arrived_ref[h] for h in range(HALVES)]
        for layer in reversed(range(layers)):
            state = [states_ref[layer, h] for h in range(HALVES)]
            back = backward_layer(layer, back, state, refs, stats_ref, dlogits_ref)

    for layer in range(layers):
        for group in range(copies_ref.shape[1]):
            copies_ref[layer, group] = dlogits_ref[layer]


def spread_kernel(normed_ref, order_ref, out_ref):
    layers, halves, tokens, half = normed_ref.shape
    rows = normed_ref[...].reshape(layers * halves * tokens, half)
    moved = jnp.dot(rows, order_ref[...], preferred_element_type=F32).astype(BF16)
    for layer in range(layers):
        for h in range(halves):
            at = (layer * halves + h) * tokens
            for group in range(out_ref.shape[1]):
                out_ref[layer, group, h] = moved[at : at + tokens, group * 128 : (group + 1) * 128]


def grad_kernel(normed_ref, dlogits_ref, out_ref):
    sources, halves, tokens, lanes = normed_ref.shape
    experts = dlogits_ref.shape[2]
    planes, rows = out_ref.shape[:2]
    dlogits = dlogits_ref[...].reshape(sources * tokens, experts)
    per_half = planes // halves
    for h in range(halves):
        normed = normed_ref[:, h].reshape(sources * tokens, lanes)
        term = lax.dot_general(normed, dlogits, (((0,), (0,)), ((), ())), preferred_element_type=F32)
        for plane in range(per_half):
            out_ref[h * per_half + plane] = term[plane * rows : (plane + 1) * rows].astype(BF16)


def call(kernel, outs, args, scratch=(), scalars=1, apart=0, apart_out=False, limit=16):
    smem = [pl.BlockSpec(memory_space=pltpu.SMEM)] * scalars
    free = pl.BlockSpec(memory_space=pltpu.HBM)
    vmem = pl.BlockSpec(memory_space=pltpu.VMEM)
    far = [pltpu.with_memory_space_constraint(arg, pltpu.HBM) for arg in args[scalars : scalars + apart]]
    args = (*args[:scalars], *far, *args[scalars + apart :])
    return pl.pallas_call(
        kernel,
        out_shape=outs,
        in_specs=smem + [free] * apart + [vmem] * (len(args) - scalars - apart),
        out_specs=jax.tree.map(lambda _: free if apart_out else vmem, outs),
        scratch_shapes=list(scratch),
        compiler_params=pltpu.CompilerParams(vmem_limit_bytes=limit * 2**20),
    )(*args)


def slot_numbers(routes):
    flattened = routes.reshape(routes.shape[0], -1)
    pair_count = flattened.shape[1]
    matches = flattened[:, :, None] == flattened[:, None, :]
    earlier = lax.broadcasted_iota(jnp.int32, (pair_count, pair_count), 1) < lax.broadcasted_iota(
        jnp.int32, (pair_count, pair_count), 0
    )
    return jnp.sum(jnp.where(matches & earlier[None], 1, 0), axis=-1).astype(jnp.int32).reshape(routes.shape)


def thirds(values):
    high = lax.reduce_precision(values, 8, 7)
    middle = lax.reduce_precision(values - high, 8, 7)
    return jnp.stack([high, middle, values - high - middle]).astype(BF16)


def from_all(rows, axis, addressed=False):
    count, here = lax.axis_size(axis), lax.axis_index(axis)
    slots = []
    for shift in range(count):
        block = lax.dynamic_index_in_dim(rows, (here + shift) % count, 0, keepdims=False) if addressed else rows
        if shift:
            block = lax.ppermute(block, axis, [(source, (source + shift) % count) for source in range(count)])
        slots.append(block)
    slots = jnp.stack(slots)
    return jnp.concatenate(
        [lax.dynamic_slice_in_dim(slots, (here - source) % count, 1, 0) for source in range(count)]
    )


def compute(expert_axes, plane_axis, flat_axes, inputs, cotangent, expert_out, route_ids, router_w, norm_gain, final_gain):
    zh = lax.axis_index("zh")
    micros, tokens, part = inputs.shape
    layers = lax.axis_size("x")
    owners = lax.axis_size(expert_axes)
    local_experts, capacity, width = expert_out.shape[2], expert_out.shape[4], expert_out.shape[5]
    half = width // HALVES
    experts = router_w.shape[2]
    choices = route_ids.shape[3]
    zh_word = jnp.reshape(zh, (1,)).astype(jnp.int32)

    crossing = jnp.where(zh == 0, cotangent, inputs)
    planes = lax.axis_size(plane_axis)
    lines = ("zh", plane_axis)
    there = [(plane, planes + (plane ^ 1)) for plane in range(planes)]
    crossed = lax.ppermute(crossing, lines, there + [(planes + plane, plane) for plane in range(planes)])
    aside = [(planes + plane, planes + (plane ^ 1)) for plane in range(planes)]
    swapped_rows = lax.ppermute(cotangent, lines, aside)
    swapped_routes = lax.ppermute(route_ids[0], lines, aside)

    row_blocks = (micros * owners, local_experts * HALVES * capacity, half)
    rows = call(
        functools.partial(layout_kernel, planes),
        jax.ShapeDtypeStruct(row_blocks, BF16),
        (zh_word, expert_out[0]),
        scratch=(
            pltpu.VMEM(expert_out.shape[1:3] + expert_out.shape[3:], BF16),
            pltpu.VMEM(row_blocks, BF16),
            pltpu.SemaphoreType.DMA((micros * local_experts,)),
            pltpu.SemaphoreType.DMA((micros * planes,)),
        ),
        apart=1,
        apart_out=True,
    )
    rows, router_here, gain_here = lax.optimization_barrier((rows, router_w[0], norm_gain[0]))
    kept = jnp.where(zh == 0, inputs, swapped_rows)
    routes_here = jnp.where(zh == 0, route_ids[0], swapped_routes)
    table = lax.all_to_all(rows, ("x",) + expert_axes, split_axis=0, concat_axis=0, tiled=True)
    table = table.reshape(layers, experts * HALVES * capacity, half)

    route_part = routes_here.astype(BF16).reshape(micros, tokens * choices // 128, 128)
    route_rows = route_part.shape[1]
    route_part = jnp.pad(route_part, ((0, 0), (0, 8 - route_rows), (0, 0)))
    act_rows = tokens * part // 128
    held = jnp.concatenate([kept.reshape(micros, act_rows, 128), route_part], axis=1)
    crossed = crossed.reshape(micros, act_rows, 128)
    lower = jnp.where(zh == 0, held[:, :act_rows], crossed)
    upper = jnp.where(zh == 0, crossed, held[:, :act_rows])
    given = jnp.concatenate([lower, upper, held[:, act_rows:]], axis=1)
    gain_part = thirds(gain_here).reshape(3 * width // 128, 128)
    gain_rows = gain_part.shape[0]
    gain_part = jnp.pad(gain_part, ((0, -gain_rows % 8), (0, 0)))
    shared = jnp.concatenate([router_here, gain_part], axis=0)
    packed = from_all(shared, "x")
    w_all = packed[:, :width]
    gain_all = packed[:, width : width + gain_rows].reshape(layers, 3, width).astype(F32)
    gain_all = (gain_all[:, 0] + gain_all[:, 1] + gain_all[:, 2]).reshape(layers, HALVES, half)
    packed = from_all(given, "x", True)
    acts = packed[:, : HALVES * act_rows].reshape(layers, HALVES, tokens, part)
    acts = acts.transpose(1, 2, 0, 3).reshape(HALVES, tokens, half)
    at = HALVES * act_rows
    routes = packed[:, at : at + route_rows].reshape(layers, tokens, choices).astype(F32).astype(jnp.int32)

    target = routes * (HALVES * capacity) + slot_numbers(routes)
    target = target.transpose(0, 2, 1)[:, None] + (jnp.arange(HALVES) * capacity)[None, :, None, None]
    target = target.reshape(layers, HALVES * choices * tokens, 1)
    select = (target == jnp.arange(experts * HALVES * capacity)[None, None, :]).astype(BF16)

    groups = owners // planes
    piece = width // owners
    feature = jnp.arange(half)
    place = feature // piece % groups * 128 + feature // (piece * groups) * piece + feature % piece
    order = (place[:, None] == jnp.arange(groups * 128)[None, :]).astype(BF16)

    shape = jax.ShapeDtypeStruct
    rows_shape = (HALVES, tokens, half)
    picks, states, stats, sent = call(
        first_kernel,
        (
            shape((layers, HALVES, choices, tokens, half), BF16),
            shape((layers,) + rows_shape, BF16),
            shape((layers, tokens, 128), F32),
            shape(rows_shape, BF16),
        ),
        (zh_word, table, select, routes, w_all, gain_all, acts),
        scratch=(
            pltpu.VMEM(table.shape, BF16),
            pltpu.VMEM(select.shape, BF16),
            pltpu.SemaphoreType.DMA((2, layers)),
        ),
        apart=2,
    )
    arrived = lax.ppermute(sent, lines, there)
    normed, dlogits, sent = call(
        middle_kernel,
        (
            shape((layers,) + rows_shape, BF16),
            shape((layers, tokens, experts), BF16),
            shape(rows_shape, BF16),
        ),
        (
            zh_word, arrived, acts, final_gain.reshape(HALVES, half), picks, routes, w_all, gain_all, states, stats,
        ),
        scratch=(pltpu.VMEM((layers,) + rows_shape, BF16), pltpu.VMEM((layers, tokens, 128), F32)),
    )
    arrived = lax.ppermute(sent, lines, [(target, source) for source, target in there])
    normed = call(
        spread_kernel, shape((layers, groups, HALVES, tokens, 128), BF16), (normed, order), scalars=0
    )
    normed = normed.reshape(layers * groups, HALVES, tokens, 128)
    normed = lax.all_to_all(normed, ("x",) + flat_axes, split_axis=0, concat_axis=0, tiled=True)
    arrived, normed = lax.optimization_barrier((arrived, normed))
    dlogits = call(
        last_kernel,
        shape((layers, groups, tokens, experts), BF16),
        (zh_word, arrived, states, stats, picks, routes, w_all, gain_all, dlogits),
        scratch=(pltpu.VMEM((layers, tokens, experts), BF16),),
    )
    dlogits = dlogits.reshape(layers * groups, tokens, experts)
    dlogits = lax.all_to_all(dlogits, ("x",) + flat_axes, split_axis=0, concat_axis=0, tiled=True)
    term = call(grad_kernel, shape((planes, piece, experts), BF16), (normed, dlogits), scalars=0)
    term = lax.all_to_all(term, plane_axis, split_axis=0, concat_axis=0, tiled=True)
    router_part = jnp.sum(term.astype(F32), axis=0)
    at = lax.axis_index(expert_axes) * (width // owners)
    w_slab = lax.dynamic_slice_in_dim(router_w[0], at, width // owners, 0).astype(F32)
    gain_slab = lax.dynamic_slice_in_dim(norm_gain[0], at, width // owners, 0)
    gain_part = jnp.sum(w_slab * router_part, axis=-1) / gain_slab
    return (router_part[None], gain_part[None])


def solution(mesh):
    sections, owners = mesh.shape["section"], mesh.shape["expert"]
    groups = 8
    planes = owners // groups
    wide = Mesh(mesh.devices.reshape(HALVES, sections // HALVES, planes, groups), ("zh", "x", "z", "yc"))
    section, expert = ("zh", "x"), ("z", "yc")
    placed = (
        P(None, expert, section),
        P(None, expert, section),
        P(section, None, expert, None, None, None),
        P(section, None, expert, None),
        P(section, None, None),
        P(section, None),
        P(),
    )
    return jax.shard_map(
        functools.partial(compute, expert, "z", ("yc",)),
        mesh=wide,
        in_specs=placed,
        out_specs=(P(section, expert, None), P(section, expert)),
        check_vma=False,
    )
```

```python
import functools

import jax
import jax.numpy as jnp
from jax import lax
from jax.experimental import pallas as pl
from jax.experimental.pallas import tpu as pltpu
from jax.sharding import Mesh, PartitionSpec as P


EPSILON = 1e-05
HALVES = 2
F32 = jnp.float32
BF16 = jnp.bfloat16


def onehots(routes_ref, layer, choices, experts):
    lanes = lax.broadcasted_iota(jnp.int32, (routes_ref.shape[1], experts), 1)
    rows = routes_ref[layer]
    return [rows[:, k : k + 1] == lanes for k in range(choices)]


def forward_layer(layer, state, refs, stats_ref, normed_ref=None):
    picks_ref, routes_ref, w_ref, gain_ref = refs
    tokens, half = state[0].shape
    experts = w_ref.shape[2]
    choices = routes_ref.shape[2]
    floats = [part.astype(F32) for part in state]
    total = sum(jnp.sum(part * part, axis=-1, keepdims=True) for part in floats)
    rscale = lax.rsqrt(total / (HALVES * half) + EPSILON)
    logits = jnp.zeros((tokens, experts), F32)
    for h in range(HALVES):
        normed = (floats[h] * rscale * gain_ref[layer, h : h + 1, :]).astype(BF16)
        if normed_ref is not None:
            normed_ref[layer, h] = normed
        logits += jnp.dot(normed, w_ref[layer, h * half : (h + 1) * half, :], preferred_element_type=F32)
    hots = onehots(routes_ref, layer, choices, experts)
    raised = [jnp.exp(jnp.sum(jnp.where(hot, logits, 0.0), axis=-1, keepdims=True)) for hot in hots]
    bottom = sum(raised)
    weights = [value / bottom for value in raised]
    lanes = lax.broadcasted_iota(jnp.int32, stats_ref.shape[1:], 1)
    stats = jnp.broadcast_to(rscale, lanes.shape)
    for k in range(choices):
        stats = jnp.where(lanes == k, weights[k], stats)
    stats_ref[layer] = stats
    fresh = []
    for h in range(HALVES):
        mixture = sum(weights[k] * picks_ref[layer, h, k].astype(F32) for k in range(choices))
        fresh.append((floats[h] + mixture).astype(BF16))
    return fresh


def backward_layer(layer, back, state, refs, stats_ref, dlogits_ref):
    picks_ref, routes_ref, w_ref, gain_ref = refs
    half = state[0].shape[1]
    experts = w_ref.shape[2]
    choices = routes_ref.shape[2]
    back_float = [part.astype(F32) for part in back]
    stats = stats_ref[layer]
    weights = [stats[:, k : k + 1] for k in range(choices)]
    rscale = stats[:, choices : choices + 1]
    dweights = [
        sum(
            jnp.sum(back_float[h] * picks_ref[layer, h, k].astype(F32), axis=-1, keepdims=True)
            for h in range(HALVES)
        )
        for k in range(choices)
    ]
    average = sum(w * d for w, d in zip(weights, dweights))
    dlogits = jnp.zeros((back[0].shape[0], experts), F32)
    for k, hot in enumerate(onehots(routes_ref, layer, choices, experts)):
        dlogits += jnp.where(hot, weights[k] * (dweights[k] - average), 0.0)
    dlogits = dlogits.astype(BF16)
    dlogits_ref[layer] = dlogits
    varied, normal = [], []
    for h in range(HALVES):
        dnormed = lax.dot_general(
            dlogits,
            w_ref[layer, h * half : (h + 1) * half, :],
            (((1,), (1,)), ((), ())),
            preferred_element_type=F32,
        )
        varied.append(dnormed * gain_ref[layer, h : h + 1, :])
        normal.append(state[h].astype(F32) * rscale)
    mean = sum(jnp.sum(v * s, axis=-1, keepdims=True) for v, s in zip(varied, normal)) / (HALVES * half)
    return [(b + rscale * (v - s * mean)).astype(BF16) for b, v, s in zip(back_float, varied, normal)]


def layout_kernel(rows_ref, out_ref, held_ref, stage_ref, in_sems, out_sems):
    micros, local_experts, owners, capacity, width = rows_ref.shape
    half = width // HALVES
    arriving = [
        [
            pltpu.make_async_copy(
                rows_ref.at[m, e], held_ref.at[m, e], in_sems.at[m * local_experts + e]
            )
            for e in range(local_experts)
        ]
        for m in range(micros)
    ]
    for copies in arriving:
        for copy in copies:
            copy.start()
    leaving = []
    for m in range(micros):
        blocks = pl.ds(m * owners, owners)
        for e in range(local_experts):
            arriving[m][e].wait()
            for h in range(HALVES):
                at = (e * HALVES + h) * capacity
                stage_ref[blocks, pl.ds(at, capacity), :] = held_ref[m, e, :, :, h * half : (h + 1) * half]
        leaving.append(pltpu.make_async_copy(stage_ref.at[blocks], out_ref.at[blocks], out_sems.at[m]))
        leaving[-1].start()
    for copy in leaving:
        copy.wait()


def pick_layer(layer, copies, table_ref, select_ref, picks_ref):
    tokens = picks_ref.shape[3]
    choices = picks_ref.shape[2]
    for copy in copies[layer]:
        copy.wait()
    rows = jnp.dot(select_ref[layer], table_ref[layer], preferred_element_type=F32).astype(BF16)
    for h in range(HALVES):
        for k in range(choices):
            at = (h * choices + k) * tokens
            picks_ref[layer, h, k] = rows[at : at + tokens]


def first_kernel(
    zh_ref, rows_ref, chosen_ref, routes_ref, w_ref, gain_ref, kept_ref, crossed_ref,
    picks_ref, states_ref, stats_ref, out_ref, table_ref, select_ref, sems,
):
    layers = table_ref.shape[0]
    copies = [
        (
            pltpu.make_async_copy(chosen_ref.at[layer], select_ref.at[layer], sems.at[0, layer]),
            pltpu.make_async_copy(rows_ref.at[layer], table_ref.at[layer], sems.at[1, layer]),
        )
        for layer in range(layers)
    ]
    for pair in copies:
        for copy in pair:
            copy.start()

    @pl.when(zh_ref[0] != 0)
    def _():
        for layer in range(layers):
            pick_layer(layer, copies, table_ref, select_ref, picks_ref)

    @pl.when(zh_ref[0] == 0)
    def _():
        refs = (picks_ref, routes_ref, w_ref, gain_ref)
        state = [kept_ref[...], crossed_ref[...]]
        for layer in range(layers):
            pick_layer(layer, copies, table_ref, select_ref, picks_ref)
            for h in range(HALVES):
                states_ref[layer, h] = state[h]
            state = forward_layer(layer, state, refs, stats_ref)
        for h in range(HALVES):
            out_ref[h] = state[h]


def middle_kernel(
    zh_ref, arrived_ref, kept_ref, crossed_ref, final_ref, picks_ref, routes_ref, w_ref, gain_ref, given_states_ref, given_stats_ref,
    normed_ref, dlogits_ref, out_ref, states_ref, stats_ref,
):
    layers = picks_ref.shape[0]
    choices = routes_ref.shape[2]
    half = kept_ref.shape[1]

    @pl.when(zh_ref[0] == 0)
    def _():
        for layer in range(layers):
            rscale = given_stats_ref[layer][:, choices : choices + 1]
            for h in range(HALVES):
                floats = given_states_ref[layer, h].astype(F32)
                normed_ref[layer, h] = (floats * rscale * gain_ref[layer, h : h + 1, :]).astype(BF16)

    @pl.when(zh_ref[0] != 0)
    def _():
        refs = (picks_ref, routes_ref, w_ref, gain_ref)
        state = [arrived_ref[h] for h in range(HALVES)]
        for layer in range(layers):
            for h in range(HALVES):
                states_ref[layer, h] = state[h]
            state = forward_layer(layer, state, refs, stats_ref, normed_ref)
        floats = [part.astype(F32) for part in state]
        total = sum(jnp.sum(part * part, axis=-1, keepdims=True) for part in floats)
        rscale = lax.rsqrt(total / (HALVES * half) + EPSILON)
        normal = [part * rscale for part in floats]
        cotangents = (crossed_ref, kept_ref)
        varied = [cotangents[h][...].astype(F32) * final_ref[h : h + 1, :] for h in range(HALVES)]
        mean = sum(jnp.sum(v * s, axis=-1, keepdims=True) for v, s in zip(varied, normal)) / (HALVES * half)
        back = [(rscale * (v - s * mean)).astype(BF16) for v, s in zip(varied, normal)]
        for layer in reversed(range(layers)):
            state = [states_ref[layer, h] for h in range(HALVES)]
            back = backward_layer(layer, back, state, refs, stats_ref, dlogits_ref)
        for h in range(HALVES):
            out_ref[h] = back[h]


def last_kernel(
    zh_ref, arrived_ref, states_ref, stats_ref, picks_ref, routes_ref, w_ref, gain_ref, given_ref,
    copies_ref, dlogits_ref,
):
    layers = picks_ref.shape[0]

    @pl.when(zh_ref[0] != 0)
    def _():
        dlogits_ref[...] = given_ref[...]

    @pl.when(zh_ref[0] == 0)
    def _():
        refs = (picks_ref, routes_ref, w_ref, gain_ref)
        back = [arrived_ref[h] for h in range(HALVES)]
        for layer in reversed(range(layers)):
            state = [states_ref[layer, h] for h in range(HALVES)]
            back = backward_layer(layer, back, state, refs, stats_ref, dlogits_ref)

    for layer in range(layers):
        for group in range(copies_ref.shape[1]):
            copies_ref[layer, group] = dlogits_ref[layer]


def spread_kernel(normed_ref, order_ref, out_ref):
    layers, halves, tokens, half = normed_ref.shape
    rows = normed_ref[...].reshape(layers * halves * tokens, half)
    moved = jnp.dot(rows, order_ref[...], preferred_element_type=F32).astype(BF16)
    for layer in range(layers):
        for h in range(halves):
            at = (layer * halves + h) * tokens
            for group in range(out_ref.shape[1]):
                out_ref[layer, group, h] = moved[at : at + tokens, group * 128 : (group + 1) * 128]


def grad_kernel(normed_ref, dlogits_ref, out_ref):
    sources, halves, tokens, lanes = normed_ref.shape
    experts = dlogits_ref.shape[2]
    planes, rows = out_ref.shape[:2]
    dlogits = dlogits_ref[...].reshape(sources * tokens, experts)
    per_half = planes // halves
    for h in range(halves):
        normed = normed_ref[:, h].reshape(sources * tokens, lanes)
        term = lax.dot_general(normed, dlogits, (((0,), (0,)), ((), ())), preferred_element_type=F32)
        for plane in range(per_half):
            out_ref[h * per_half + plane] = term[plane * rows : (plane + 1) * rows].astype(BF16)


def call(kernel, outs, args, scratch=(), scalars=1, apart=0, apart_out=False, limit=16):
    smem = [pl.BlockSpec(memory_space=pltpu.SMEM)] * scalars
    free = pl.BlockSpec(memory_space=pltpu.HBM)
    vmem = pl.BlockSpec(memory_space=pltpu.VMEM)
    far = [pltpu.with_memory_space_constraint(arg, pltpu.HBM) for arg in args[scalars : scalars + apart]]
    args = (*args[:scalars], *far, *args[scalars + apart :])
    return pl.pallas_call(
        kernel,
        out_shape=outs,
        in_specs=smem + [free] * apart + [vmem] * (len(args) - scalars - apart),
        out_specs=jax.tree.map(lambda _: free if apart_out else vmem, outs),
        scratch_shapes=list(scratch),
        compiler_params=pltpu.CompilerParams(vmem_limit_bytes=limit * 2**20),
    )(*args)


def slot_numbers(routes):
    flattened = routes.reshape(routes.shape[0], -1)
    pair_count = flattened.shape[1]
    matches = flattened[:, :, None] == flattened[:, None, :]
    earlier = lax.broadcasted_iota(jnp.int32, (pair_count, pair_count), 1) < lax.broadcasted_iota(
        jnp.int32, (pair_count, pair_count), 0
    )
    return jnp.sum(jnp.where(matches & earlier[None], 1, 0), axis=-1).astype(jnp.int32).reshape(routes.shape)


def thirds(values):
    high = lax.reduce_precision(values, 8, 7)
    middle = lax.reduce_precision(values - high, 8, 7)
    return jnp.stack([high, middle, values - high - middle]).astype(BF16)


def from_all(rows, axis, addressed=False):
    count, here = lax.axis_size(axis), lax.axis_index(axis)
    slots = []
    for shift in range(count):
        block = lax.dynamic_index_in_dim(rows, (here + shift) % count, 0, keepdims=False) if addressed else rows
        if shift:
            block = lax.ppermute(block, axis, [(source, (source + shift) % count) for source in range(count)])
        slots.append(block)
    slots = jnp.stack(slots)
    return jnp.concatenate(
        [lax.dynamic_slice_in_dim(slots, (here - source) % count, 1, 0) for source in range(count)]
    )


def compute(expert_axes, plane_axis, flat_axes, inputs, cotangent, expert_out, route_ids, router_w, norm_gain, final_gain):
    zh = lax.axis_index("zh")
    micros, tokens, part = inputs.shape
    layers = lax.axis_size("x")
    owners = lax.axis_size(expert_axes)
    local_experts, capacity, width = expert_out.shape[2], expert_out.shape[4], expert_out.shape[5]
    half = width // HALVES
    experts = router_w.shape[2]
    choices = route_ids.shape[3]
    zh_word = jnp.reshape(zh, (1,)).astype(jnp.int32)

    row_blocks = (micros * owners, local_experts * HALVES * capacity, half)
    rows = call(
        layout_kernel,
        jax.ShapeDtypeStruct(row_blocks, BF16),
        (expert_out[0],),
        scratch=(
            pltpu.VMEM(expert_out.shape[1:3] + expert_out.shape[3:], BF16),
            pltpu.VMEM(row_blocks, BF16),
            pltpu.SemaphoreType.DMA((micros * local_experts,)),
            pltpu.SemaphoreType.DMA((micros,)),
        ),
        scalars=0,
        apart=1,
        apart_out=True,
    )
    rows, router_here, gain_here, routes_here, inputs, cotangent = lax.optimization_barrier(
        (rows, router_w[0], norm_gain[0], route_ids[0], inputs, cotangent)
    )
    table = lax.all_to_all(rows, ("x",) + expert_axes, split_axis=0, concat_axis=0, tiled=True)
    table = table.reshape(layers, experts * HALVES * capacity, half)

    route_part = routes_here.astype(BF16).reshape(micros, tokens * choices // 128, 128)
    route_rows = route_part.shape[1]
    route_part = jnp.pad(route_part, ((0, 0), (0, 8 - route_rows), (0, 0)))
    act_rows = tokens * part // 128
    pair = jnp.stack([inputs, cotangent], axis=1).reshape(micros, HALVES * act_rows, 128)
    given = jnp.concatenate([pair, route_part], axis=1)
    gain_part = thirds(gain_here).reshape(3 * width // 128, 128)
    gain_rows = gain_part.shape[0]
    gain_part = jnp.pad(gain_part, ((0, -gain_rows % 8), (0, 0)))
    shared = jnp.concatenate([router_here, gain_part], axis=0)
    packed = from_all(given, "x", True)
    pair = packed[:, : HALVES * act_rows].reshape(layers, HALVES, tokens, part)
    pair = pair.transpose(1, 2, 0, 3).reshape(HALVES, tokens, half)
    kept = jnp.where(zh == 0, pair[0], pair[1])
    crossed = lax.ppermute(jnp.where(zh == 0, pair[1], pair[0]), "zh", [(0, 1), (1, 0)])
    at = HALVES * act_rows
    routes = packed[:, at : at + route_rows].reshape(layers, tokens, choices).astype(F32).astype(jnp.int32)
    packed = from_all(shared, "x")
    w_all = packed[:, :width]
    gain_all = packed[:, width : width + gain_rows].reshape(layers, 3, width).astype(F32)
    gain_all = (gain_all[:, 0] + gain_all[:, 1] + gain_all[:, 2]).reshape(layers, HALVES, half)

    target = routes * (HALVES * capacity) + slot_numbers(routes)
    target = target.transpose(0, 2, 1)[:, None] + (jnp.arange(HALVES) * capacity)[None, :, None, None]
    target = target.reshape(layers, HALVES * choices * tokens, 1)
    select = (target == jnp.arange(experts * HALVES * capacity)[None, None, :]).astype(BF16)

    planes = lax.axis_size(plane_axis)
    groups = owners // planes
    piece = width // owners
    feature = jnp.arange(half)
    place = feature // piece % groups * 128 + feature // (piece * groups) * piece + feature % piece
    order = (place[:, None] == jnp.arange(groups * 128)[None, :]).astype(BF16)

    shape = jax.ShapeDtypeStruct
    rows_shape = (HALVES, tokens, half)
    picks, states, stats, sent = call(
        first_kernel,
        (
            shape((layers, HALVES, choices, tokens, half), BF16),
            shape((layers,) + rows_shape, BF16),
            shape((layers, tokens, 128), F32),
            shape(rows_shape, BF16),
        ),
        (zh_word, table, select, routes, w_all, gain_all, kept, crossed),
        scratch=(
            pltpu.VMEM(table.shape, BF16),
            pltpu.VMEM(select.shape, BF16),
            pltpu.SemaphoreType.DMA((2, layers)),
        ),
        apart=2,
    )
    arrived = lax.ppermute(sent, "zh", [(0, 1)])
    normed, dlogits, sent = call(
        middle_kernel,
        (
            shape((layers,) + rows_shape, BF16),
            shape((layers, tokens, experts), BF16),
            shape(rows_shape, BF16),
        ),
        (
            zh_word, arrived, kept, crossed, final_gain.reshape(HALVES, half), picks, routes, w_all, gain_all, states, stats,
        ),
        scratch=(pltpu.VMEM((layers,) + rows_shape, BF16), pltpu.VMEM((layers, tokens, 128), F32)),
    )
    arrived = lax.ppermute(sent, "zh", [(1, 0)])
    normed = call(
        spread_kernel, shape((layers, groups, HALVES, tokens, 128), BF16), (normed, order), scalars=0
    )
    normed = normed.reshape(layers * groups, HALVES, tokens, 128)
    normed = lax.all_to_all(normed, ("x",) + flat_axes, split_axis=0, concat_axis=0, tiled=True)
    arrived, normed = lax.optimization_barrier((arrived, normed))
    dlogits = call(
        last_kernel,
        shape((layers, groups, tokens, experts), BF16),
        (zh_word, arrived, states, stats, picks, routes, w_all, gain_all, dlogits),
        scratch=(pltpu.VMEM((layers, tokens, experts), BF16),),
    )
    dlogits = dlogits.reshape(layers * groups, tokens, experts)
    dlogits = lax.all_to_all(dlogits, ("x",) + flat_axes, split_axis=0, concat_axis=0, tiled=True)
    term = call(grad_kernel, shape((planes, piece, experts), BF16), (normed, dlogits), scalars=0)
    term = lax.all_to_all(term, plane_axis, split_axis=0, concat_axis=0, tiled=True)
    router_part = jnp.sum(term.astype(F32), axis=0)
    at = lax.axis_index(expert_axes) * (width // owners)
    w_slab = lax.dynamic_slice_in_dim(router_w[0], at, width // owners, 0).astype(F32)
    gain_slab = lax.dynamic_slice_in_dim(norm_gain[0], at, width // owners, 0)
    gain_part = jnp.sum(w_slab * router_part, axis=-1) / gain_slab
    return (router_part[None], gain_part[None])


def solution(mesh):
    sections, owners = mesh.shape["section"], mesh.shape["expert"]
    groups = 8
    planes = owners // groups
    wide = Mesh(mesh.devices.reshape(HALVES, sections // HALVES, planes, groups), ("zh", "x", "z", "yc"))
    section, expert = ("zh", "x"), ("z", "yc")
    placed = (
        P(None, expert, section),
        P(None, expert, section),
        P(section, None, expert, None, None, None),
        P(section, None, expert, None),
        P(section, None, None),
        P(section, None),
        P(),
    )
    return jax.shard_map(
        functools.partial(compute, expert, "z", ("yc",)),
        mesh=wide,
        in_specs=placed,
        out_specs=(P(section, expert, None), P(section, expert)),
        check_vma=False,
    )
```

```python
import functools

import jax
import jax.numpy as jnp
from jax import lax
from jax.experimental import pallas as pl
from jax.experimental.pallas import tpu as pltpu
from jax.sharding import Mesh, PartitionSpec as P


EPSILON = 1e-05
HALVES = 2
F32 = jnp.float32
BF16 = jnp.bfloat16


def onehots(routes_ref, layer, choices, experts):
    lanes = lax.broadcasted_iota(jnp.int32, (routes_ref.shape[1], experts), 1)
    rows = routes_ref[layer]
    return [rows[:, k : k + 1] == lanes for k in range(choices)]


def forward_layer(layer, state, refs, stats_ref, normed_ref=None):
    picks_ref, routes_ref, w_ref, gain_ref = refs
    tokens, half = state[0].shape
    experts = w_ref.shape[2]
    choices = routes_ref.shape[2]
    floats = [part.astype(F32) for part in state]
    total = sum(jnp.sum(part * part, axis=-1, keepdims=True) for part in floats)
    rscale = lax.rsqrt(total / (HALVES * half) + EPSILON)
    logits = jnp.zeros((tokens, experts), F32)
    for h in range(HALVES):
        normed = (floats[h] * rscale * gain_ref[layer, h : h + 1, :]).astype(BF16)
        if normed_ref is not None:
            normed_ref[layer, h] = normed
        logits += jnp.dot(normed, w_ref[layer, h * half : (h + 1) * half, :], preferred_element_type=F32)
    hots = onehots(routes_ref, layer, choices, experts)
    raised = [jnp.exp(jnp.sum(jnp.where(hot, logits, 0.0), axis=-1, keepdims=True)) for hot in hots]
    bottom = sum(raised)
    weights = [value / bottom for value in raised]
    lanes = lax.broadcasted_iota(jnp.int32, stats_ref.shape[1:], 1)
    stats = jnp.broadcast_to(rscale, lanes.shape)
    for k in range(choices):
        stats = jnp.where(lanes == k, weights[k], stats)
    stats_ref[layer] = stats
    fresh = []
    for h in range(HALVES):
        mixture = sum(weights[k] * picks_ref[layer, h, k].astype(F32) for k in range(choices))
        fresh.append((floats[h] + mixture).astype(BF16))
    return fresh


def backward_layer(layer, back, state, refs, stats_ref, dlogits_ref):
    picks_ref, routes_ref, w_ref, gain_ref = refs
    half = state[0].shape[1]
    experts = w_ref.shape[2]
    choices = routes_ref.shape[2]
    back_float = [part.astype(F32) for part in back]
    stats = stats_ref[layer]
    weights = [stats[:, k : k + 1] for k in range(choices)]
    rscale = stats[:, choices : choices + 1]
    dweights = [
        sum(
            jnp.sum(back_float[h] * picks_ref[layer, h, k].astype(F32), axis=-1, keepdims=True)
            for h in range(HALVES)
        )
        for k in range(choices)
    ]
    average = sum(w * d for w, d in zip(weights, dweights))
    dlogits = jnp.zeros((back[0].shape[0], experts), F32)
    for k, hot in enumerate(onehots(routes_ref, layer, choices, experts)):
        dlogits += jnp.where(hot, weights[k] * (dweights[k] - average), 0.0)
    dlogits = dlogits.astype(BF16)
    dlogits_ref[layer] = dlogits
    varied, normal = [], []
    for h in range(HALVES):
        dnormed = lax.dot_general(
            dlogits,
            w_ref[layer, h * half : (h + 1) * half, :],
            (((1,), (1,)), ((), ())),
            preferred_element_type=F32,
        )
        varied.append(dnormed * gain_ref[layer, h : h + 1, :])
        normal.append(state[h].astype(F32) * rscale)
    mean = sum(jnp.sum(v * s, axis=-1, keepdims=True) for v, s in zip(varied, normal)) / (HALVES * half)
    return [(b + rscale * (v - s * mean)).astype(BF16) for b, v, s in zip(back_float, varied, normal)]


def layout_kernel(rows_ref, out_ref, held_ref, stage_ref, in_sems, out_sems):
    micros, local_experts, owners, capacity, width = rows_ref.shape
    half = width // HALVES
    arriving = [
        [
            pltpu.make_async_copy(
                rows_ref.at[m, e], held_ref.at[m, e], in_sems.at[m * local_experts + e]
            )
            for e in range(local_experts)
        ]
        for m in range(micros)
    ]
    for copies in arriving:
        for copy in copies:
            copy.start()
    leaving = []
    for m in range(micros):
        blocks = pl.ds(m * owners, owners)
        for e in range(local_experts):
            arriving[m][e].wait()
            for h in range(HALVES):
                at = (e * HALVES + h) * capacity
                stage_ref[blocks, pl.ds(at, capacity), :] = held_ref[m, e, :, :, h * half : (h + 1) * half]
        leaving.append(pltpu.make_async_copy(stage_ref.at[blocks], out_ref.at[blocks], out_sems.at[m]))
        leaving[-1].start()
    for copy in leaving:
        copy.wait()


def pick_layer(layer, copies, table_ref, select_ref, picks_ref):
    tokens = picks_ref.shape[3]
    choices = picks_ref.shape[2]
    for copy in copies[layer]:
        copy.wait()
    rows = jnp.dot(select_ref[layer], table_ref[layer], preferred_element_type=F32).astype(BF16)
    for h in range(HALVES):
        for k in range(choices):
            at = (h * choices + k) * tokens
            picks_ref[layer, h, k] = rows[at : at + tokens]


def first_kernel(
    zh_ref, rows_ref, chosen_ref, routes_ref, w_ref, gain_ref, kept_ref, crossed_ref,
    picks_ref, kept_states_ref, stats_ref, out_ref, table_ref, select_ref, states_ref, sems, state_sems,
):
    layers = table_ref.shape[0]
    copies = [
        (
            pltpu.make_async_copy(chosen_ref.at[layer], select_ref.at[layer], sems.at[0, layer]),
            pltpu.make_async_copy(rows_ref.at[layer], table_ref.at[layer], sems.at[1, layer]),
        )
        for layer in range(layers)
    ]
    for pair in copies:
        for copy in pair:
            copy.start()

    @pl.when(zh_ref[0] != 0)
    def _():
        for layer in range(layers):
            pick_layer(layer, copies, table_ref, select_ref, picks_ref)

    @pl.when(zh_ref[0] == 0)
    def _():
        refs = (picks_ref, routes_ref, w_ref, gain_ref)
        state = [kept_ref[...], crossed_ref[...]]
        leaving = []
        for layer in range(layers):
            pick_layer(layer, copies, table_ref, select_ref, picks_ref)
            for h in range(HALVES):
                states_ref[layer, h] = state[h]
            leaving.append(
                pltpu.make_async_copy(states_ref.at[layer], kept_states_ref.at[layer], state_sems.at[layer])
            )
            leaving[-1].start()
            state = forward_layer(layer, state, refs, stats_ref)
        for h in range(HALVES):
            out_ref[h] = state[h]
        for copy in leaving:
            copy.wait()


def middle_kernel(
    zh_ref, given_states_ref, arrived_ref, kept_ref, crossed_ref, final_ref, picks_ref, routes_ref, w_ref, gain_ref,
    given_stats_ref, normed_ref, dlogits_ref, out_ref, states_ref, stats_ref, sem,
):
    layers = picks_ref.shape[0]
    choices = routes_ref.shape[2]
    half = kept_ref.shape[1]

    @pl.when(zh_ref[0] == 0)
    def _():
        copy = pltpu.make_async_copy(given_states_ref, states_ref, sem)
        copy.start()
        copy.wait()
        for layer in range(layers):
            rscale = given_stats_ref[layer][:, choices : choices + 1]
            for h in range(HALVES):
                floats = states_ref[layer, h].astype(F32)
                normed_ref[layer, h] = (floats * rscale * gain_ref[layer, h : h + 1, :]).astype(BF16)

    @pl.when(zh_ref[0] != 0)
    def _():
        refs = (picks_ref, routes_ref, w_ref, gain_ref)
        state = [arrived_ref[h] for h in range(HALVES)]
        for layer in range(layers):
            for h in range(HALVES):
                states_ref[layer, h] = state[h]
            state = forward_layer(layer, state, refs, stats_ref, normed_ref)
        floats = [part.astype(F32) for part in state]
        total = sum(jnp.sum(part * part, axis=-1, keepdims=True) for part in floats)
        rscale = lax.rsqrt(total / (HALVES * half) + EPSILON)
        normal = [part * rscale for part in floats]
        cotangents = (crossed_ref, kept_ref)
        varied = [cotangents[h][...].astype(F32) * final_ref[h : h + 1, :] for h in range(HALVES)]
        mean = sum(jnp.sum(v * s, axis=-1, keepdims=True) for v, s in zip(varied, normal)) / (HALVES * half)
        back = [(rscale * (v - s * mean)).astype(BF16) for v, s in zip(varied, normal)]
        for layer in reversed(range(layers)):
            state = [states_ref[layer, h] for h in range(HALVES)]
            back = backward_layer(layer, back, state, refs, stats_ref, dlogits_ref)
        for h in range(HALVES):
            out_ref[h] = back[h]


def last_kernel(
    zh_ref, kept_states_ref, arrived_ref, stats_ref, picks_ref, routes_ref, w_ref, gain_ref, given_ref,
    copies_ref, dlogits_ref, states_ref, sems,
):
    layers = picks_ref.shape[0]

    @pl.when(zh_ref[0] != 0)
    def _():
        dlogits_ref[...] = given_ref[...]

    @pl.when(zh_ref[0] == 0)
    def _():
        refs = (picks_ref, routes_ref, w_ref, gain_ref)
        back = [arrived_ref[h] for h in range(HALVES)]
        arriving = [
            pltpu.make_async_copy(kept_states_ref.at[layer], states_ref.at[layer], sems.at[layer])
            for layer in range(layers)
        ]
        for copy in reversed(arriving):
            copy.start()
        for layer in reversed(range(layers)):
            arriving[layer].wait()
            state = [states_ref[layer, h] for h in range(HALVES)]
            back = backward_layer(layer, back, state, refs, stats_ref, dlogits_ref)

    for layer in range(layers):
        for group in range(copies_ref.shape[1]):
            copies_ref[layer, group] = dlogits_ref[layer]


def spread_kernel(normed_ref, order_ref, out_ref):
    layers, halves, tokens, half = normed_ref.shape
    rows = normed_ref[...].reshape(layers * halves * tokens, half)
    moved = jnp.dot(rows, order_ref[...], preferred_element_type=F32).astype(BF16)
    for layer in range(layers):
        for h in range(halves):
            at = (layer * halves + h) * tokens
            for group in range(out_ref.shape[1]):
                out_ref[layer, group, h] = moved[at : at + tokens, group * 128 : (group + 1) * 128]


def grad_kernel(normed_ref, dlogits_ref, out_ref):
    sources, halves, tokens, lanes = normed_ref.shape
    experts = dlogits_ref.shape[2]
    planes, rows = out_ref.shape[:2]
    dlogits = dlogits_ref[...].reshape(sources * tokens, experts)
    per_half = planes // halves
    for h in range(halves):
        normed = normed_ref[:, h].reshape(sources * tokens, lanes)
        term = lax.dot_general(normed, dlogits, (((0,), (0,)), ((), ())), preferred_element_type=F32)
        for plane in range(per_half):
            out_ref[h * per_half + plane] = term[plane * rows : (plane + 1) * rows].astype(BF16)


def call(kernel, outs, args, scratch=(), scalars=1, apart=0, apart_out=(), limit=16):
    smem = [pl.BlockSpec(memory_space=pltpu.SMEM)] * scalars
    free = pl.BlockSpec(memory_space=pltpu.HBM)
    vmem = pl.BlockSpec(memory_space=pltpu.VMEM)
    far = [pltpu.with_memory_space_constraint(arg, pltpu.HBM) for arg in args[scalars : scalars + apart]]
    args = (*args[:scalars], *far, *args[scalars + apart :])
    single = not isinstance(outs, tuple)
    outs = (outs,) if single else outs
    results = pl.pallas_call(
        kernel,
        out_shape=[pltpu.HBM(out.shape, out.dtype) if index in apart_out else out for index, out in enumerate(outs)],
        in_specs=smem + [free] * apart + [vmem] * (len(args) - scalars - apart),
        out_specs=[free if index in apart_out else vmem for index in range(len(outs))],
        scratch_shapes=list(scratch),
        compiler_params=pltpu.CompilerParams(vmem_limit_bytes=limit * 2**20),
    )(*args)
    return results[0] if single else results


def slot_numbers(routes):
    flattened = routes.reshape(routes.shape[0], -1)
    pair_count = flattened.shape[1]
    matches = flattened[:, :, None] == flattened[:, None, :]
    earlier = lax.broadcasted_iota(jnp.int32, (pair_count, pair_count), 1) < lax.broadcasted_iota(
        jnp.int32, (pair_count, pair_count), 0
    )
    return jnp.sum(jnp.where(matches & earlier[None], 1, 0), axis=-1).astype(jnp.int32).reshape(routes.shape)


def thirds(values):
    high = lax.reduce_precision(values, 8, 7)
    middle = lax.reduce_precision(values - high, 8, 7)
    return jnp.stack([high, middle, values - high - middle]).astype(BF16)


def from_all(rows, axis, addressed=False):
    count, here = lax.axis_size(axis), lax.axis_index(axis)
    slots = []
    for shift in range(count):
        block = lax.dynamic_index_in_dim(rows, (here + shift) % count, 0, keepdims=False) if addressed else rows
        if shift:
            block = lax.ppermute(block, axis, [(source, (source + shift) % count) for source in range(count)])
        slots.append(block)
    slots = jnp.stack(slots)
    return jnp.concatenate(
        [lax.dynamic_slice_in_dim(slots, (here - source) % count, 1, 0) for source in range(count)]
    )


def compute(expert_axes, plane_axis, flat_axes, inputs, cotangent, expert_out, route_ids, router_w, norm_gain, final_gain):
    zh = lax.axis_index("zh")
    micros, tokens, part = inputs.shape
    layers = lax.axis_size("x")
    owners = lax.axis_size(expert_axes)
    local_experts, capacity, width = expert_out.shape[2], expert_out.shape[4], expert_out.shape[5]
    half = width // HALVES
    experts = router_w.shape[2]
    choices = route_ids.shape[3]
    zh_word = jnp.reshape(zh, (1,)).astype(jnp.int32)

    row_blocks = (micros * owners, local_experts * HALVES * capacity, half)
    rows = call(
        layout_kernel,
        jax.ShapeDtypeStruct(row_blocks, BF16),
        (expert_out[0],),
        scratch=(
            pltpu.VMEM(expert_out.shape[1:3] + expert_out.shape[3:], BF16),
            pltpu.VMEM(row_blocks, BF16),
            pltpu.SemaphoreType.DMA((micros * local_experts,)),
            pltpu.SemaphoreType.DMA((micros,)),
        ),
        scalars=0,
        apart=1,
        apart_out=(0,),
    )
    rows, router_here, gain_here, routes_here, inputs, cotangent = lax.optimization_barrier(
        (rows, router_w[0], norm_gain[0], route_ids[0], inputs, cotangent)
    )
    table = lax.all_to_all(rows, ("x",) + expert_axes, split_axis=0, concat_axis=0, tiled=True)
    table = table.reshape(layers, experts * HALVES * capacity, half)

    route_part = routes_here.astype(BF16).reshape(micros, tokens * choices // 128, 128)
    route_rows = route_part.shape[1]
    route_part = jnp.pad(route_part, ((0, 0), (0, 8 - route_rows), (0, 0)))
    act_rows = tokens * part // 128
    pair = jnp.stack([inputs, cotangent], axis=1).reshape(micros, HALVES * act_rows, 128)
    given = jnp.concatenate([pair, route_part], axis=1)
    gain_part = thirds(gain_here).reshape(3 * width // 128, 128)
    gain_rows = gain_part.shape[0]
    gain_part = jnp.pad(gain_part, ((0, -gain_rows % 8), (0, 0)))
    shared = jnp.concatenate([router_here, gain_part], axis=0)
    packed = from_all(given, "x", True)
    pair = packed[:, : HALVES * act_rows].reshape(layers, HALVES, tokens, part)
    pair = pair.transpose(1, 2, 0, 3).reshape(HALVES, tokens, half)
    kept = jnp.where(zh == 0, pair[0], pair[1])
    crossed = lax.ppermute(jnp.where(zh == 0, pair[1], pair[0]), "zh", [(0, 1), (1, 0)])
    at = HALVES * act_rows
    routes = packed[:, at : at + route_rows].reshape(layers, tokens, choices).astype(F32).astype(jnp.int32)
    packed = from_all(shared, "x")
    w_all = packed[:, :width]
    gain_all = packed[:, width : width + gain_rows].reshape(layers, 3, width).astype(F32)
    gain_all = (gain_all[:, 0] + gain_all[:, 1] + gain_all[:, 2]).reshape(layers, HALVES, half)

    target = routes * (HALVES * capacity) + slot_numbers(routes)
    target = target.transpose(0, 2, 1)[:, None] + (jnp.arange(HALVES) * capacity)[None, :, None, None]
    target = target.reshape(layers, HALVES * choices * tokens, 1)
    select = (target == jnp.arange(experts * HALVES * capacity)[None, None, :]).astype(BF16)

    planes = lax.axis_size(plane_axis)
    groups = owners // planes
    piece = width // owners
    feature = jnp.arange(half)
    place = feature // piece % groups * 128 + feature // (piece * groups) * piece + feature % piece
    order = (place[:, None] == jnp.arange(groups * 128)[None, :]).astype(BF16)

    shape = jax.ShapeDtypeStruct
    rows_shape = (HALVES, tokens, half)
    picks, states, stats, sent = call(
        first_kernel,
        (
            shape((layers, HALVES, choices, tokens, half), BF16),
            shape((layers,) + rows_shape, BF16),
            shape((layers, tokens, 128), F32),
            shape(rows_shape, BF16),
        ),
        (zh_word, table, select, routes, w_all, gain_all, kept, crossed),
        scratch=(
            pltpu.VMEM(table.shape, BF16),
            pltpu.VMEM(select.shape, BF16),
            pltpu.VMEM((layers,) + rows_shape, BF16),
            pltpu.SemaphoreType.DMA((2, layers)),
            pltpu.SemaphoreType.DMA((layers,)),
        ),
        apart=2,
        apart_out=(1,),
    )
    arrived = lax.ppermute(sent, "zh", [(0, 1)])
    normed, dlogits, sent = call(
        middle_kernel,
        (
            shape((layers,) + rows_shape, BF16),
            shape((layers, tokens, experts), BF16),
            shape(rows_shape, BF16),
        ),
        (
            zh_word, states, arrived, kept, crossed, final_gain.reshape(HALVES, half), picks, routes, w_all, gain_all, stats,
        ),
        scratch=(
            pltpu.VMEM((layers,) + rows_shape, BF16),
            pltpu.VMEM((layers, tokens, 128), F32),
            pltpu.SemaphoreType.DMA,
        ),
        apart=1,
    )
    arrived = lax.ppermute(sent, "zh", [(1, 0)])
    normed = call(
        spread_kernel, shape((layers, groups, HALVES, tokens, 128), BF16), (normed, order), scalars=0
    )
    normed = normed.reshape(layers * groups, HALVES, tokens, 128)
    normed = lax.all_to_all(normed, ("x",) + flat_axes, split_axis=0, concat_axis=0, tiled=True)
    arrived, normed = lax.optimization_barrier((arrived, normed))
    dlogits = call(
        last_kernel,
        shape((layers, groups, tokens, experts), BF16),
        (zh_word, states, arrived, stats, picks, routes, w_all, gain_all, dlogits),
        scratch=(
            pltpu.VMEM((layers, tokens, experts), BF16),
            pltpu.VMEM((layers,) + rows_shape, BF16),
            pltpu.SemaphoreType.DMA((layers,)),
        ),
        apart=1,
    )
    dlogits = dlogits.reshape(layers * groups, tokens, experts)
    dlogits = lax.all_to_all(dlogits, ("x",) + flat_axes, split_axis=0, concat_axis=0, tiled=True)
    term = call(grad_kernel, shape((planes, piece, experts), BF16), (normed, dlogits), scalars=0)
    term = lax.all_to_all(term, plane_axis, split_axis=0, concat_axis=0, tiled=True)
    router_part = jnp.sum(term.astype(F32), axis=0)
    at = lax.axis_index(expert_axes) * (width // owners)
    w_slab = lax.dynamic_slice_in_dim(router_w[0], at, width // owners, 0).astype(F32)
    gain_slab = lax.dynamic_slice_in_dim(norm_gain[0], at, width // owners, 0)
    gain_part = jnp.sum(w_slab * router_part, axis=-1) / gain_slab
    return (router_part[None], gain_part[None])


def solution(mesh):
    sections, owners = mesh.shape["section"], mesh.shape["expert"]
    groups = 8
    planes = owners // groups
    wide = Mesh(mesh.devices.reshape(HALVES, sections // HALVES, planes, groups), ("zh", "x", "z", "yc"))
    section, expert = ("zh", "x"), ("z", "yc")
    placed = (
        P(None, expert, section),
        P(None, expert, section),
        P(section, None, expert, None, None, None),
        P(section, None, expert, None),
        P(section, None, None),
        P(section, None),
        P(),
    )
    return jax.shard_map(
        functools.partial(compute, expert, "z", ("yc",)),
        mesh=wide,
        in_specs=placed,
        out_specs=(P(section, expert, None), P(section, expert)),
        check_vma=False,
    )
```
